128 devices in a mesh: row: 8 (over x, core), col: 16 (over z, y).
Axes of the slice: x: 4, y: 4, z: 4, core: 2. Of those that a mesh axis runs over, the one named last changes fastest.
Arguments:
- trailing: float32 [24576, 24576], P('row', 'col'), may hold values from -6 to 6
- panel_first: float32 [24576, 256], P(('row', 'col')), may hold values from -0.0390625 to 0.0390625
- panel_second: float32 [24576, 256], P(('row', 'col')), may hold values from -0.0390625 to 0.0390625
- link_block: float32 [256, 256], replicated, may hold values from -0.375 to 0.375
- inverse_first: float32 [256, 256], replicated, may hold values from -6 to 6
- inverse_second: float32 [256, 256], replicated, may hold values from -6 to 6
- tile_struct: int32 [2, 192], replicated, may hold values 0 or 1
Outputs:
- panel_out_first: float32 [24576, 256], P(('row', 'col'))
- diag_out_first: float32 [256, 256], replicated
- panel_out_second: float32 [24576, 256], P(('row', 'col'))
- cross_out_second: float32 [256, 256], replicated
- diag_out_second: float32 [256, 256], replicated
The draws below stay inside these ranges and needn't reach their ends.
All inputs are finite; a program needn't handle non-finite values.
Results may differ from the reference program's by a relative error of at most 0.000071.
Values sent between devices are 32-bit elements; how exact they have to be, the bound alone decides.
A program may use at most 128 MiB of HBM per device.

```python
import jax
import jax.numpy as jnp
from jax import lax

M = 24576
W = 256
TILE = 128
TILES = 192


def set_ends(result, stream_key, low, high):
    longest = result.shape.index(max(result.shape))
    spots = []
    for shift in (0, 1):
        where = [jax.random.randint(jax.random.fold_in(stream_key, axis), (), 0, length) for axis, length in enumerate(result.shape)]
        where[longest] = (where[longest] + shift) % result.shape[longest]
        spots.append(tuple(where))
    return result.at[spots[0]].set(low).at[spots[1]].set(high)


def with_spikes(values, own_key, source, target, shards_of, factor):
    def block_of(position):
        return (jnp.arange(values.shape[position]) // (values.shape[position] // shards_of)).reshape((-1,) + (1,) * (values.ndim - 1 - position))

    near = jax.random.permutation(own_key, shards_of)[block_of(target)]
    far = (block_of(target) + shards_of // 2) % shards_of
    return jnp.where((block_of(source) == near) | (block_of(source) == far), factor * values, values)


def levels(key, dims, cuts, smallest, largest):
    level, own = 1.0, jax.random.fold_in(key, 6)
    for position, blocks in cuts:
        steps = jnp.exp(jax.random.uniform(jax.random.fold_in(own, position), (blocks,), jnp.float32, smallest / len(cuts), largest / len(cuts)))
        level = level * jnp.repeat(steps, dims[position] // blocks).reshape([-1 if axis == position else 1 for axis in range(len(dims))])
    return level


def centred(key, dims, scale, limit, cuts=(), kind=jnp.bfloat16):
    loudness = levels(key, dims, cuts, -0.22, 0.18) if cuts else 1.0
    array = jax.random.normal(key, dims, jnp.float32) * scale * loudness
    return jnp.minimum(jnp.maximum(array, -limit), limit).astype(kind)


def noise_with(own_key, dims, width, bound, split, heavy, kind=jnp.bfloat16):
    values = width * jax.random.normal(own_key, dims, jnp.float32)
    if split:
        values = values * levels(own_key, dims, split, -0.22, 0.18)
    return jnp.clip(with_spikes(values, jax.random.fold_in(own_key, 3), *heavy), -bound, bound).astype(kind)


def setup_inputs(seed: int = 0) -> dict:
    splits = jax.random.split(jax.random.key(seed), 8)
    trailing = noise_with(splits[0], (M, M), 1.0, 6.0, ((0, 8), (1, 16)), (1, 0, 16, 2.0), jnp.float32)
    panel_first = centred(splits[1], (M, W), M ** -0.5, 0.0390625, ((0, 128),), jnp.float32)
    panel_second = centred(splits[2], (M, W), M ** -0.5, 0.0390625, ((0, 128),), jnp.float32)
    link_block = centred(splits[3], (W, W), W ** -0.5, 0.375, (), jnp.float32)
    inverse_first = centred(splits[4], (W, W), 1.0, 6.0, (), jnp.float32)
    inverse_second = centred(splits[5], (W, W), 1.0, 6.0, (), jnp.float32)
    tile_struct = set_ends((jax.random.randint(splits[6], (2, TILES), 0, 4) < 3).astype(jnp.int32), jax.random.fold_in(splits[6], 1), 0, 1)
    return {"trailing": trailing, "panel_first": panel_first, "panel_second": panel_second, "link_block": link_block, "inverse_first": inverse_first, "inverse_second": inverse_second, "tile_struct": tile_struct}


def matmul(left, right):
    return jnp.dot(left, right, precision=lax.Precision.HIGHEST, preferred_element_type=jnp.float32)


def reference(trailing, panel_first, panel_second, link_block, inverse_first, inverse_second, tile_struct):
    row_mask = jnp.repeat(tile_struct, TILE, axis=1).astype(jnp.float32)
    lead_first = panel_first * row_mask[0][:, None]
    lead_second = panel_second * row_mask[1][:, None]
    panel_out_first = -matmul(trailing, lead_first)
    diag_out_first = inverse_first - matmul(lead_first.T, panel_out_first)
    reach = matmul(trailing, lead_second)
    panel_out_second = -(matmul(panel_out_first, link_block) + reach)
    cross_out_second = -(matmul(diag_out_first, link_block) + matmul(panel_out_first.T, lead_second))
    diag_out_second = inverse_second - matmul(link_block.T, cross_out_second) - matmul(lead_second.T, panel_out_second)
    return panel_out_first, diag_out_first, panel_out_second, cross_out_second, diag_out_second
```

```python
import functools

import jax
import jax.numpy as jnp
from jax import lax
from jax.experimental import pallas as pl
from jax.experimental.pallas import tpu as pltpu
from jax.sharding import Mesh
from jax.sharding import PartitionSpec as P

AXES = ("x", "core", "z", "y")
MESH = pl.DeviceIdType.MESH
ROWS = 192
W = 256
HALF = 128
DEPTH = 1536
SUMS = 3 * W
PART = SUMS // 32

UNITS = (
    [(2, 2), (2, 3), (2, 0), (2, 1)]
    + [(3, 2), (0, 2), (1, 2)]
    + [(1, 1), (1, 3), (3, 1), (3, 3)]
    + [(1, 0), (3, 0), (0, 1), (0, 3), (0, 0)]
)
PLACE = {unit: i for i, unit in enumerate(UNITS)}


def route(near, far):
    if near == 0:
        return "keep", 0
    if near == 2:
        return "relay", 1 if far % 2 == 0 else -1
    if near == 1:
        return ("joined" if far % 2 == 0 else "own"), 1
    return ("joined" if far % 2 == 1 else "own"), -1


def split(value):
    high = value.astype(jnp.bfloat16)
    return high, (value - high.astype(jnp.float32)).astype(jnp.bfloat16)


def dot(left, right):
    return jnp.dot(left, right, preferred_element_type=jnp.float32)


def exact(left, right, contract=(1, 0)):
    return lax.dot_general(
        left,
        right,
        (((contract[0],), (contract[1],)), ((), ())),
        precision=lax.Precision.HIGHEST,
        preferred_element_type=jnp.float32,
    )


def kernel(
    struct, trailing, first, second, link_in, inv1_in, inv2_in,
    out1, diag1, out2, cross2, diag2,
    t_buf, raw, lead_h, lead_l, prod_a, prod_b, got_a, got_b, far_a, far_b,
    lead, link, inv1, inv2, y_buf,
    sums, sum_p, sum_q, sum_x, total,
    t_sem, in_sem, g1_send, g1_recv, g2_send, g2_recv, g3_send, g3_recv,
    r_send, r_recv, f_send, f_recv, s_send, s_recv,
):
    x, k, z, y = (lax.axis_index(name) for name in AXES)
    c = z * 4 + y
    flat = (x * 2 + k) * 16 + c
    panels = (first, second)

    def at(dx=0, dk=0, dz=0, dy=0):
        return (
            lax.rem(x + dx + 4, 4) if dx else x,
            1 - k if dk else k,
            lax.rem(z + dz + 4, 4) if dz else z,
            lax.rem(y + dy + 4, 4) if dy else y,
        )

    def remote(src, dst, send, recv, where):
        return pltpu.make_async_remote_copy(
            src_ref=src, dst_ref=dst, send_sem=send, recv_sem=recv, device_id=where, device_id_type=MESH
        )

    def t_copy(u, start=None):
        dy, dz = UNITS[u]
        block = lax.rem(z + dz, 4) * 4 + lax.rem(y + dy, 4)
        return pltpu.make_async_copy(
            trailing.at[pl.ds(pl.multiple_of(block * ROWS, ROWS), ROWS)], t_buf.at[u], t_sem.at[u]
        )

    own_copies = [
        pltpu.make_async_copy(first, lead.at[0], in_sem.at[0]),
        pltpu.make_async_copy(second, lead.at[1], in_sem.at[1]),
        pltpu.make_async_copy(link_in, link, in_sem.at[2]),
        pltpu.make_async_copy(inv1_in, inv1, in_sem.at[3]),
        pltpu.make_async_copy(inv2_in, inv2, in_sem.at[4]),
    ]
    for copy in own_copies:
        copy.start()
    for u in range(16):
        t_copy(u).start()

    target = [(q, lax.rem(z, 2), x, 2 * k + lax.div(z, 2)) for q in range(4)]
    source = [(z, lax.div(y, 2), 2 * lax.rem(y, 2) + k, i) for i in range(4)]
    at_home = (z == x) & (k == lax.rem(z, 2)) & (y == 2 * k + lax.div(z, 2))
    plane = [(o // 4, o % 4) for o in range(1, 16)]
    barrier = pltpu.get_barrier_semaphore()

    def greet(where):
        pl.semaphore_signal(barrier, inc=1, device_id=where, device_id_type=MESH)

    mate = at(dk=1)
    for i in range(4):
        for where, same in ((target[i], at_home & (x == i)), (source[i], at_home & (y == i))):
            greet(tuple(jnp.where(same, there, here) for there, here in zip(mate, where)))
    for dx in (1, 2, 3):
        greet(at(dx=dx))
    greet(at(dk=1))
    for dz, dy in plane:
        greet(at(dz=dz, dy=dy))
    mate_home = (z == x) & (1 - k == lax.rem(z, 2)) & (y == 2 * (1 - k) + lax.div(z, 2))
    pl.semaphore_wait(barrier, 27 + 2 * mate_home.astype(jnp.int32) - 2 * at_home.astype(jnp.int32))

    def quarter(p, q):
        slot = raw.at[p, lax.rem(z, 2) * 4 + y, pl.ds(q * 48, 48)]
        return remote(panels[p].at[pl.ds(q * 48, 48)], slot, g1_send.at[p, q], g1_recv.at[p, y], target[q])

    def quarter_home(p, q):
        slot = raw.at[p, lax.rem(z, 2) * 4 + y, pl.ds(q * 48, 48)]
        return pltpu.make_async_copy(panels[p].at[pl.ds(q * 48, 48)], slot, g1_recv.at[p, y])

    for p in range(2):
        for q in range(4):
            same = at_home & (x == q)

            @pl.when(same)
            def _(p=p, q=q):
                quarter_home(p, q).start()

            @pl.when(jnp.logical_not(same))
            def _(p=p, q=q):
                quarter(p, q).start()

    for copy in own_copies:
        copy.wait()
    for p in range(2):
        for s in range(3):
            rows = pl.ds(64 * s, 64)
            mask = struct[p, lax.div(flat * 3 + s, 2)].astype(jnp.float32)
            lead[p, rows] = lead[p, rows] * mask

    def pieces(p, lo, n, dx):
        q = lax.rem(x + dx + 4, 4)
        return raw.at[p, pl.ds(4 * k + lo, n), pl.ds(pl.multiple_of(q * 48, 48), 48)]

    def ring(p, way, m):
        step = 1 if way == 0 else -1
        lo = (0, 2, 0)[m] if way == 0 else (2, 0, 2)[m]
        ref = pieces(p, lo, 2, -step if m == 2 else 0)
        return remote(ref, ref, g2_send.at[p, way, m], g2_recv.at[p, way, m], at(dx=step))

    def ring_wait(p, way, m):
        step = 1 if way == 0 else -1
        lo = (0, 2, 0)[m] if way == 0 else (2, 0, 2)[m]
        ref = pieces(p, lo, 2, -2 * step if m == 2 else -step)
        remote(ref, ref, g2_send.at[p, way, m], g2_recv.at[p, way, m], at(dx=step)).wait_recv()

    def across(p, m):
        ref = pieces(p, 0, 4, (0, -1, 1, 2)[m])
        return remote(ref, ref, g3_send.at[p, m], g3_recv.at[p, m], at(dk=1))

    def across_wait(p, m):
        q = lax.rem(x + (0, -1, 1, 2)[m] + 4, 4)
        ref = raw.at[p, pl.ds(4 * (1 - k), 4), pl.ds(pl.multiple_of(q * 48, 48), 48)]
        remote(ref, ref, g3_send.at[p, m], g3_recv.at[p, m], at(dk=1)).wait_recv()

    def gather_1(p):
        for i in range(4):
            ref = raw.at[p, 4 * k + i, pl.ds(pl.multiple_of(x * 48, 48), 48)]
            pltpu.make_async_copy(ref, ref, g1_recv.at[p, i]).wait()
        for m in range(2):
            for way in range(2):
                ring(p, way, m).start()
        across(p, 0).start()

    def gather_2(p):
        for way in range(2):
            ring_wait(p, way, 0)
            ring(p, way, 2).start()

    def gather_3(p):
        for way in range(2):
            ring_wait(p, way, 1)
            across(p, 1 + way).start()

    def gather_4(p):
        for way in range(2):
            ring_wait(p, way, 2)
        across(p, 3).start()

    def gather_5(p):
        for m in range(4):
            across_wait(p, m)

        @pl.loop(0, 8)
        def _(j):
            for s in range(3):
                mask = struct[p, lax.div((c * 8 + j) * 3 + s, 2)].astype(jnp.float32)
                high, low = split(raw[p, j, pl.ds(64 * s, 64)] * mask)
                rows = pl.ds(pl.multiple_of(j * ROWS + 64 * s, 64), 64)
                lead_h[p, rows] = high
                lead_l[p, rows] = low

    def pick(h):
        return (prod_a, got_a, far_a) if h == 0 else (prod_b, got_b, far_b)

    def roles(h, unit):
        dy, dz = unit
        near, far = (dy, dz) if h == 0 else (dz, dy)
        return near, far, *route(near, far)

    def next_to(h, way, phase=1):
        along_y = (h == 0) == (phase == 1)
        return at(dy=way) if along_y else at(dz=way)

    def hop(p, h, unit):
        near, far, kind, way = roles(h, unit)
        prod, got, _ = pick(h)
        slot = 0 if kind == "relay" else (1 if way == 1 else 2)
        return remote(
            prod.at[p, PLACE[unit]], got.at[p, slot, far], r_send.at[p, h, slot, far], r_recv.at[p, h, slot, far],
            next_to(h, way),
        )

    def hop_wait(p, h, slot, far):
        _, got, _ = pick(h)
        ref = got.at[p, slot, far]
        remote(ref, ref, r_send.at[p, h, slot, far], r_recv.at[p, h, slot, far], next_to(h, 1)).wait_recv()

    def unit_of(h, near, far):
        return (near, far) if h == 0 else (far, near)

    def compute(p, lo, hi):
        @pl.loop(lo, hi)
        def _(u):
            if p == 0:
                for v in range(lo, hi):

                    @pl.when(u == v)
                    def _(v=v):
                        t_copy(v).wait()

            high, low = split(t_buf[u])
            wide = (dot(high, lead_h[p]) + dot(low, lead_h[p])) + dot(high, lead_l[p])
            prod_a[p, u] = wide[:, :HALF]
            prod_b[p, u] = wide[:, HALF:]
            for v in range(lo, hi):
                sends = [h for h in range(2) if roles(h, UNITS[v])[2] in ("relay", "own")]
                if sends:

                    @pl.when(u == v)
                    def _(v=v, sends=sends):
                        for h in sends:
                            hop(p, h, UNITS[v]).start()

    def joined(p, h):
        prod, got, _ = pick(h)
        for near, far in ((1, 0), (1, 2), (3, 1), (3, 3)):
            unit = unit_of(h, near, far)
            hop_wait(p, h, 0, far)
            prod[p, PLACE[unit]] = prod[p, PLACE[unit]] + got[p, 0, far]
            hop(p, h, unit).start()

    def second_send(p, h, far):
        prod, _, got = pick(h)
        return remote(
            prod.at[p, PLACE[unit_of(h, 0, far)]], got.at[p, far - 1], f_send.at[p, h, far - 1],
            f_recv.at[p, h, far - 1], next_to(h, far, phase=2),
        )

    def second_phase(p, h):
        prod, got, _ = pick(h)
        for far in (2, 1, 3, 0):
            u = PLACE[unit_of(h, 0, far)]
            hop_wait(p, h, 1, far)
            hop_wait(p, h, 2, far)
            prod[p, u] = prod[p, u] + (got[p, 1, far] + got[p, 2, far])
            if far:
                second_send(p, h, far).start()

    def finish(p, h):
        prod, _, got = pick(h)
        for far in (1, 2, 3):
            ref = got.at[p, far - 1]
            remote(ref, ref, f_send.at[p, h, far - 1], f_recv.at[p, h, far - 1], next_to(h, far, 2)).wait_recv()
        value = (prod[p, PLACE[(0, 0)]] + got[p, 0]) + (got[p, 1] + got[p, 2])
        y_buf[p, :, pl.ds(h * HALF, HALF)] = value

    def rows_of(core, place):
        return pl.ds(pl.multiple_of(core * (SUMS // 2) + place * PART, 8), PART)

    def half_of(core):
        return pl.ds(pl.multiple_of(core * (SUMS // 2), 8), SUMS // 2)

    def reduce_all():
        swap = remote(sums.at[half_of(1 - k)], sum_p, s_send.at[0], s_recv.at[0], at(dk=1))
        swap.start()
        swap.wait_recv()
        sums[half_of(k)] = sums[half_of(k)] + sum_p[...]
        for o, (dz, dy) in enumerate(plane):
            where = at(dz=dz, dy=dy)
            remote(
                sums.at[rows_of(k, where[2] * 4 + where[3])], sum_q.at[o], s_send.at[1], s_recv.at[1], where
            ).start()
        remote(sum_q, sum_q, s_send.at[1], s_recv.at[1], at(dk=1)).wait_recv()
        value = sums[rows_of(k, c)]
        for o in range(15):
            value = value + sum_q[o]
        sum_x[x] = value
        cross = [
            remote(sum_x.at[x], sum_x.at[x], s_send.at[1 + dx], s_recv.at[1 + dx], at(dx=dx)) for dx in (1, 2, 3)
        ]
        for copy in cross:
            copy.start()
        for dx in (1, 2, 3):
            ref = sum_x.at[lax.rem(x - dx + 4, 4)]
            remote(ref, ref, s_send.at[1 + dx], s_recv.at[1 + dx], at(dx=dx)).wait_recv()
        mine = rows_of(k, c)
        total[mine] = (sum_x[0] + sum_x[1]) + (sum_x[2] + sum_x[3])
        for dz, dy in plane:
            remote(total.at[mine], total.at[mine], s_send.at[5], s_recv.at[5], at(dz=dz, dy=dy)).start()
        remote(sum_q, sum_q, s_send.at[5], s_recv.at[5], at(dk=1)).wait_recv()
        back = remote(total.at[half_of(k)], total.at[half_of(k)], s_send.at[6], s_recv.at[6], at(dk=1))
        back.start()
        ref = total.at[half_of(1 - k)]
        remote(ref, ref, s_send.at[6], s_recv.at[6], at(dk=1)).wait_recv()
        swap.wait_send()
        remote(sum_q, sum_q, s_send.at[1], s_recv.at[1], at(dk=1)).wait_send()
        for copy in cross:
            copy.wait_send()
        remote(sum_q, sum_q, s_send.at[5], s_recv.at[5], at(dk=1)).wait_send()
        back.wait_send()

    gather_1(0)
    gather_2(0)
    gather_3(0)
    gather_4(0)
    gather_5(0)
    compute(0, 0, 4)
    gather_1(1)
    compute(0, 4, 7)
    gather_2(1)
    compute(0, 7, 11)
    gather_3(1)
    gather_4(1)
    compute(0, 11, 16)
    joined(0, 0)
    joined(0, 1)
    gather_5(1)
    compute(1, 0, 4)
    compute(1, 4, 7)
    second_phase(0, 0)
    compute(1, 7, 11)
    second_phase(0, 1)
    compute(1, 11, 16)
    joined(1, 0)
    joined(1, 1)
    finish(0, 0)
    finish(0, 1)
    out1[...] = -y_buf[0]
    out2[...] = exact(y_buf[0], link[...])
    for p in range(2):
        sums[pl.ds(p * W, W)] = exact(lead[p], y_buf[0], (0, 0))
    second_phase(1, 0)
    second_phase(1, 1)
    finish(1, 0)
    finish(1, 1)
    out2[...] = out2[...] - y_buf[1]
    sums[pl.ds(2 * W, W)] = exact(lead[1], y_buf[1], (0, 0))
    reduce_all()
    diag1[...] = inv1[...] + total[pl.ds(0, W)]
    cross2[...] = jnp.transpose(total[pl.ds(W, W)]) - exact(diag1[...], link[...])
    diag2[...] = (
        (inv2[...] - exact(link[...], cross2[...], (0, 0))) - exact(total[pl.ds(W, W)], link[...])
    ) + total[pl.ds(2 * W, W)]

    for p in range(2):
        for q in range(4):

            @pl.when(jnp.logical_not(at_home & (x == q)))
            def _(p=p, q=q):
                quarter(p, q).wait_send()

        for way in range(2):
            for m in range(3):
                ring(p, way, m).wait_send()
        for m in range(4):
            across(p, m).wait_send()
        for h in range(2):
            for unit in UNITS:
                if roles(h, unit)[2] != "keep":
                    hop(p, h, unit).wait_send()
            for far in (1, 2, 3):
                second_send(p, h, far).wait_send()


def on_device(trailing, first, second, link, inv1, inv2, struct):
    f32, bf16 = jnp.float32, jnp.bfloat16
    square = jax.ShapeDtypeStruct((W, W), f32)
    tall = jax.ShapeDtypeStruct((ROWS, W), f32)
    vmem, anywhere = pl.BlockSpec(memory_space=pltpu.VMEM), pl.BlockSpec(memory_space=pl.ANY)
    dma = pltpu.SemaphoreType.DMA
    block = (ROWS, HALF)
    return pl.pallas_call(
        kernel,
        out_shape=(tall, square, tall, square, square),
        in_specs=[pl.BlockSpec(memory_space=pltpu.SMEM)] + [anywhere] * 6,
        out_specs=(vmem,) * 5,
        scratch_shapes=[
            pltpu.VMEM((16, ROWS, DEPTH), f32),
            pltpu.VMEM((2, 8, ROWS, W), f32),
            pltpu.VMEM((2, DEPTH, W), bf16),
            pltpu.VMEM((2, DEPTH, W), bf16),
            pltpu.VMEM((2, 16, *block), f32),
            pltpu.VMEM((2, 16, *block), f32),
            pltpu.VMEM((2, 3, 4, *block), f32),
            pltpu.VMEM((2, 3, 4, *block), f32),
            pltpu.VMEM((2, 3, *block), f32),
            pltpu.VMEM((2, 3, *block), f32),
            pltpu.VMEM((2, ROWS, W), f32),
            pltpu.VMEM((W, W), f32),
            pltpu.VMEM((W, W), f32),
            pltpu.VMEM((W, W), f32),
            pltpu.VMEM((2, ROWS, W), f32),
            pltpu.VMEM((SUMS, W), f32),
            pltpu.VMEM((SUMS // 2, W), f32),
            pltpu.VMEM((15, PART, W), f32),
            pltpu.VMEM((4, PART, W), f32),
            pltpu.VMEM((SUMS, W), f32),
            dma((16,)), dma((5,)), dma((2, 4)), dma((2, 4)), dma((2, 2, 3)), dma((2, 2, 3)), dma((2, 4)), dma((2, 4)),
            dma((2, 2, 3, 4)), dma((2, 2, 3, 4)), dma((2, 2, 3)), dma((2, 2, 3)), dma((7,)), dma((7,)),
        ],
        compiler_params=pltpu.CompilerParams(
            collective_id=0, has_side_effects=True, vmem_limit_bytes=60 * 1024 * 1024
        ),
        name="selected_inversion",
    )(struct, trailing, first, second, link, inv1, inv2)


def solution(mesh):
    finer = Mesh(mesh.devices.reshape(4, 2, 4, 4), AXES)
    row, col = ("x", "core"), ("z", "y")
    both = (*row, *col)
    in_specs = (P(row, col), P(both, None), P(both, None), P(), P(), P(), P())
    out_specs = (P(both, None), P(), P(both, None), P(), P())
    return jax.shard_map(on_device, mesh=finer, in_specs=in_specs, out_specs=out_specs, check_vma=False)
```

```python
import jax
import jax.numpy as jnp
from jax import lax
from jax.experimental import pallas as pl
from jax.experimental.pallas import tpu as pltpu
from jax.sharding import Mesh
from jax.sharding import PartitionSpec as P

AXES = ("x", "core", "z", "y")
MESH = pl.DeviceIdType.MESH
ROWS = 192
W = 256
HALF = 128
DEPTH = 1536

UNITS = (
    [(2, 2), (2, 3), (3, 2), (2, 1), (1, 2), (2, 0), (0, 2)]
    + [(1, 1), (1, 3), (3, 1), (1, 0), (0, 1)]
    + [(3, 3), (3, 0), (0, 3), (0, 0)]
)
PLACE = {unit: i for i, unit in enumerate(UNITS)}


def route(near, far):
    if near == 0:
        return "keep", 0
    if near == 2:
        return "relay", 1 if far % 2 == 0 else -1
    if near == 1:
        return ("joined" if far % 2 == 0 else "own"), 1
    return ("joined" if far % 2 == 1 else "own"), -1


def split(value):
    high = value.astype(jnp.bfloat16)
    return high, (value - high.astype(jnp.float32)).astype(jnp.bfloat16)


def dot(left, right):
    return jnp.dot(left, right, preferred_element_type=jnp.float32)


def exact(left, right, contract=(1, 0)):
    return lax.dot_general(
        left,
        right,
        (((contract[0],), (contract[1],)), ((), ())),
        precision=lax.Precision.HIGHEST,
        preferred_element_type=jnp.float32,
    )


def kernel(
    struct, trailing, first, second, link_in, inv1_in, inv2_in,
    out1, diag1, out2, cross2, diag2,
    t_buf, raw, lead_h, lead_l, prod_a, prod_b, got_a, got_b, far_a, far_b,
    lead, link, inv1, inv2, y_buf,
    sums, sum_p, sum_x, sum_q, total, tail, tail_p, tail_q, tail_x, last,
    t_sem, in_sem, g1_send, g1_recv, g2_send, g2_recv, g3_send, g3_recv,
    r_send, r_recv, f_send, f_recv, s_send, s_recv, e_send, e_recv,
):
    x, k, z, y = (lax.axis_index(name) for name in AXES)
    c = z * 4 + y
    flat = (x * 2 + k) * 16 + c
    panels = (first, second)

    def at(dx=0, dk=0, dz=0, dy=0):
        return (
            lax.rem(x + dx + 4, 4) if dx else x,
            1 - k if dk else k,
            lax.rem(z + dz + 4, 4) if dz else z,
            lax.rem(y + dy + 4, 4) if dy else y,
        )

    def remote(src, dst, send, recv, where):
        return pltpu.make_async_remote_copy(
            src_ref=src, dst_ref=dst, send_sem=send, recv_sem=recv, device_id=where, device_id_type=MESH
        )

    def t_copy(u, start=None):
        dy, dz = UNITS[u]
        block = lax.rem(z + dz, 4) * 4 + lax.rem(y + dy, 4)
        return pltpu.make_async_copy(
            trailing.at[pl.ds(pl.multiple_of(block * ROWS, ROWS), ROWS)], t_buf.at[u], t_sem.at[u]
        )

    own_copies = [
        pltpu.make_async_copy(first, lead.at[0], in_sem.at[0]),
        pltpu.make_async_copy(second, lead.at[1], in_sem.at[1]),
        pltpu.make_async_copy(link_in, link, in_sem.at[2]),
        pltpu.make_async_copy(inv1_in, inv1, in_sem.at[3]),
        pltpu.make_async_copy(inv2_in, inv2, in_sem.at[4]),
    ]
    for copy in own_copies:
        copy.start()
    for u in range(16):
        t_copy(u).start()

    target = [(q, lax.rem(z, 2), x, 2 * k + lax.div(z, 2)) for q in range(4)]
    source = [(z, lax.div(y, 2), 2 * lax.rem(y, 2) + k, i) for i in range(4)]
    at_home = (z == x) & (k == lax.rem(z, 2)) & (y == 2 * k + lax.div(z, 2))
    plane = [(o // 4, o % 4) for o in range(1, 16)]
    barrier = pltpu.get_barrier_semaphore()

    def greet(where):
        pl.semaphore_signal(barrier, inc=1, device_id=where, device_id_type=MESH)

    mate = at(dk=1)
    for i in range(4):
        for where, same in ((target[i], at_home & (x == i)), (source[i], at_home & (y == i))):
            greet(tuple(jnp.where(same, there, here) for there, here in zip(mate, where)))
    for dx in (1, 2, 3):
        greet(at(dx=dx))
    greet(at(dk=1))
    for dz, dy in plane:
        greet(at(dz=dz, dy=dy))
    mate_home = (z == x) & (1 - k == lax.rem(z, 2)) & (y == 2 * (1 - k) + lax.div(z, 2))
    pl.semaphore_wait(barrier, 27 + 2 * mate_home.astype(jnp.int32) - 2 * at_home.astype(jnp.int32))

    def quarter(p, q):
        slot = raw.at[p, lax.rem(z, 2) * 4 + y, pl.ds(q * 48, 48)]
        return remote(panels[p].at[pl.ds(q * 48, 48)], slot, g1_send.at[p, q], g1_recv.at[p, y], target[q])

    def quarter_home(p, q):
        slot = raw.at[p, lax.rem(z, 2) * 4 + y, pl.ds(q * 48, 48)]
        return pltpu.make_async_copy(panels[p].at[pl.ds(q * 48, 48)], slot, g1_recv.at[p, y])

    def gather_0(p):
        for q in range(4):
            same = at_home & (x == q)

            @pl.when(same)
            def _(p=p, q=q):
                quarter_home(p, q).start()

            @pl.when(jnp.logical_not(same))
            def _(p=p, q=q):
                quarter(p, q).start()

    gather_0(0)
    for copy in own_copies:
        copy.wait()
    for p in range(2):
        for s in range(3):
            rows = pl.ds(64 * s, 64)
            mask = struct[p, lax.div(flat * 3 + s, 2)].astype(jnp.float32)
            lead[p, rows] = lead[p, rows] * mask

    def pieces(p, lo, n, dx):
        q = lax.rem(x + dx + 4, 4)
        return raw.at[p, pl.ds(4 * k + lo, n), pl.ds(pl.multiple_of(q * 48, 48), 48)]

    def ring(p, way, m):
        step = 1 if way == 0 else -1
        lo = (0, 2, 0)[m] if way == 0 else (2, 0, 2)[m]
        ref = pieces(p, lo, 2, -step if m == 2 else 0)
        return remote(ref, ref, g2_send.at[p, way, m], g2_recv.at[p, way, m], at(dx=step))

    def ring_wait(p, way, m):
        step = 1 if way == 0 else -1
        lo = (0, 2, 0)[m] if way == 0 else (2, 0, 2)[m]
        ref = pieces(p, lo, 2, -2 * step if m == 2 else -step)
        remote(ref, ref, g2_send.at[p, way, m], g2_recv.at[p, way, m], at(dx=step)).wait_recv()

    def across(p, m):
        ref = pieces(p, 0, 4, (0, -1, 1, 2)[m])
        return remote(ref, ref, g3_send.at[p, m], g3_recv.at[p, m], at(dk=1))

    def across_wait(p, m):
        q = lax.rem(x + (0, -1, 1, 2)[m] + 4, 4)
        ref = raw.at[p, pl.ds(4 * (1 - k), 4), pl.ds(pl.multiple_of(q * 48, 48), 48)]
        remote(ref, ref, g3_send.at[p, m], g3_recv.at[p, m], at(dk=1)).wait_recv()

    def gather_1(p):
        for i in range(4):
            ref = raw.at[p, 4 * k + i, pl.ds(pl.multiple_of(x * 48, 48), 48)]
            pltpu.make_async_copy(ref, ref, g1_recv.at[p, i]).wait()
        for m in range(2):
            for way in range(2):
                ring(p, way, m).start()
        across(p, 0).start()

    def gather_2(p):
        for way in range(2):
            ring_wait(p, way, 0)
            ring(p, way, 2).start()

    def gather_3(p):
        for way in range(2):
            ring_wait(p, way, 1)
            across(p, 1 + way).start()

    def gather_4(p):
        for way in range(2):
            ring_wait(p, way, 2)
        across(p, 3).start()

    def gather_5(p):
        for m in range(4):
            across_wait(p, m)

        @pl.loop(0, 8)
        def _(j):
            for s in range(3):
                mask = struct[p, lax.div((c * 8 + j) * 3 + s, 2)].astype(jnp.float32)
                high, low = split(raw[p, j, pl.ds(64 * s, 64)] * mask)
                rows = pl.ds(pl.multiple_of(j * ROWS + 64 * s, 64), 64)
                lead_h[p, rows] = high
                lead_l[p, rows] = low

    def pick(h):
        return (prod_a, got_a, far_a) if h == 0 else (prod_b, got_b, far_b)

    def roles(h, unit):
        dy, dz = unit
        near, far = (dy, dz) if h == 0 else (dz, dy)
        return near, far, *route(near, far)

    def next_to(h, way, phase=1):
        along_y = (h == 0) == (phase == 1)
        return at(dy=way) if along_y else at(dz=way)

    def hop(p, h, unit):
        near, far, kind, way = roles(h, unit)
        prod, got, _ = pick(h)
        slot = 0 if kind == "relay" else (1 if way == 1 else 2)
        return remote(
            prod.at[p, PLACE[unit]], got.at[p, slot, far], r_send.at[p, h, slot, far], r_recv.at[p, h, slot, far],
            next_to(h, way),
        )

    def hop_wait(p, h, slot, far):
        _, got, _ = pick(h)
        ref = got.at[p, slot, far]
        remote(ref, ref, r_send.at[p, h, slot, far], r_recv.at[p, h, slot, far], next_to(h, 1)).wait_recv()

    def unit_of(h, near, far):
        return (near, far) if h == 0 else (far, near)

    def compute(p, lo, hi):
        @pl.loop(lo, hi)
        def _(u):
            if p == 0:
                for v in range(lo, hi):

                    @pl.when(u == v)
                    def _(v=v):
                        t_copy(v).wait()

            high, low = split(t_buf[u])
            wide = (dot(high, lead_h[p]) + dot(low, lead_h[p])) + dot(high, lead_l[p])
            prod_a[p, u] = wide[:, :HALF]
            prod_b[p, u] = wide[:, HALF:]
            for v in range(lo, hi):
                sends = [h for h in range(2) if roles(h, UNITS[v])[2] in ("relay", "own")]
                if sends:

                    @pl.when(u == v)
                    def _(v=v, sends=sends):
                        for h in sends:
                            hop(p, h, UNITS[v]).start()

    def joined(p, far):
        for h in range(2):
            prod, got, _ = pick(h)
            unit = unit_of(h, 1 if far % 2 == 0 else 3, far)
            hop_wait(p, h, 0, far)
            prod[p, PLACE[unit]] = prod[p, PLACE[unit]] + got[p, 0, far]
            hop(p, h, unit).start()

    def second_send(p, h, far):
        prod, _, got = pick(h)
        return remote(
            prod.at[p, PLACE[unit_of(h, 0, far)]], got.at[p, far - 1], f_send.at[p, h, far - 1],
            f_recv.at[p, h, far - 1], next_to(h, far, phase=2),
        )

    def second_phase(p, far):
        for h in range(2):
            prod, got, _ = pick(h)
            u = PLACE[unit_of(h, 0, far)]
            hop_wait(p, h, 1, far)
            hop_wait(p, h, 2, far)
            prod[p, u] = prod[p, u] + (got[p, 1, far] + got[p, 2, far])
            if far:
                second_send(p, h, far).start()

    def finish(p, h):
        prod, _, got = pick(h)
        for far in (1, 2, 3):
            ref = got.at[p, far - 1]
            remote(ref, ref, f_send.at[p, h, far - 1], f_recv.at[p, h, far - 1], next_to(h, far, 2)).wait_recv()
        value = (prod[p, PLACE[(0, 0)]] + got[p, 0]) + (got[p, 1] + got[p, 2])
        y_buf[p, :, pl.ds(h * HALF, HALF)] = value

    def rows(ref, start, size):
        return ref.at[pl.ds(pl.multiple_of(start, 8), size)]

    def sent(src, dst, i, where):
        return remote(src, dst, s_send.at[i], s_recv.at[i], where)

    def spot(ref, start, place):
        row = pl.multiple_of(start + 8 * lax.div(place, 2), 8)
        return ref.at[pl.ds(row, 8), pl.ds(pl.multiple_of(lax.rem(place, 2) * HALF, HALF), HALF)]

    quart = k * W + x * 64

    def early_swap(core):
        return sent(rows(sums, core * W, W), sum_p, 0, at(dk=1))

    def early_x(dx):
        there = lax.rem(x + dx, 4)
        return sent(rows(sums, k * W + there * 64, 64), sum_x.at[dx - 1], dx, at(dx=dx))

    def early_plane(o):
        dz, dy = plane[o]
        where = at(dz=dz, dy=dy)
        return sent(spot(sums, quart, where[2] * 4 + where[3]), sum_q.at[o], 4, where)

    def early_spread(o):
        dz, dy = plane[o]
        mine = spot(total, quart, c)
        return sent(mine, mine, 5, at(dz=dz, dy=dy))

    def early_spread_x(dx):
        mine = rows(total, quart, 64)
        return sent(mine, mine, 5 + dx, at(dx=dx))

    def early_back(core):
        half = rows(total, core * W, W)
        return sent(half, half, 9, at(dk=1))

    def early(step):
        if step == 0:
            early_swap(1 - k).start()
        if step == 1:
            early_swap(1 - k).wait_recv()
            half = rows(sums, k * W, W)
            half[...] = half[...] + sum_p[...]
            for dx in (2, 1, 3):
                early_x(dx).start()
        if step == 2:
            for dx in (1, 2, 3):
                early_x(dx).wait_recv()
            mine = rows(sums, quart, 64)
            mine[...] = (mine[...] + sum_x[0]) + (sum_x[1] + sum_x[2])
            for o in range(15):
                early_plane(o).start()
        if step == 3:
            sent(sum_q, sum_q, 4, at(dk=1)).wait_recv()
            value = spot(sums, quart, c)[...]
            for o in range(15):
                value = value + sum_q[o]
            spot(total, quart, c)[...] = value
            for o in range(15):
                early_spread(o).start()
        if step == 4:
            sent(sum_q, sum_q, 5, at(dk=1)).wait_recv()
            for dx in (2, 1, 3):
                early_spread_x(dx).start()
        if step == 5:
            for dx in (1, 2, 3):
                ref = rows(total, k * W + lax.rem(x - dx + 4, 4) * 64, 64)
                sent(ref, ref, 5 + dx, at(dx=dx)).wait_recv()
            early_back(k).start()
        if step == 6:
            early_back(1 - k).wait_recv()

    def late_sent(src, dst, i, where):
        return remote(src, dst, e_send.at[i], e_recv.at[i], where)

    def late_swap(core):
        return late_sent(rows(tail, core * HALF, HALF), tail_p, 0, at(dk=1))

    def late_plane(o):
        dz, dy = plane[o]
        where = at(dz=dz, dy=dy)
        return late_sent(rows(tail, k * HALF + 8 * (where[2] * 4 + where[3]), 8), tail_q.at[o], 1, where)

    def late_x(dx):
        return late_sent(tail_x.at[x], tail_x.at[x], 1 + dx, at(dx=dx))

    def late_spread(o):
        dz, dy = plane[o]
        mine = rows(last, k * HALF + 8 * c, 8)
        return late_sent(mine, mine, 5, at(dz=dz, dy=dy))

    def late_back(core):
        half = rows(last, core * HALF, HALF)
        return late_sent(half, half, 6, at(dk=1))

    def late(step):
        if step == 0:
            late_swap(1 - k).start()
        if step == 1:
            late_swap(1 - k).wait_recv()
            half = rows(tail, k * HALF, HALF)
            half[...] = half[...] + tail_p[...]
            for o in range(15):
                late_plane(o).start()
        if step == 2:
            late_sent(tail_q, tail_q, 1, at(dk=1)).wait_recv()
            value = rows(tail, k * HALF + 8 * c, 8)[...]
            for o in range(15):
                value = value + tail_q[o]
            tail_x[x] = value
            for dx in (2, 1, 3):
                late_x(dx).start()
        if step == 3:
            for dx in (1, 2, 3):
                ref = tail_x.at[lax.rem(x - dx + 4, 4)]
                late_sent(ref, ref, 1 + dx, at(dx=dx)).wait_recv()
            rows(last, k * HALF + 8 * c, 8)[...] = (tail_x[0] + tail_x[1]) + (tail_x[2] + tail_x[3])
            for o in range(15):
                late_spread(o).start()
        if step == 4:
            late_sent(tail_q, tail_q, 5, at(dk=1)).wait_recv()
            late_back(k).start()
        if step == 5:
            late_back(1 - k).wait_recv()

    gather_1(0)
    gather_2(0)
    gather_3(0)
    gather_4(0)
    gather_0(1)
    gather_5(0)
    compute(0, 0, 7)
    compute(0, 7, 12)
    gather_1(1)
    joined(0, 2)
    joined(0, 1)
    compute(0, 12, 16)
    gather_2(1)
    joined(0, 3)
    joined(0, 0)
    gather_3(1)
    gather_4(1)
    second_phase(0, 2)
    gather_5(1)
    compute(1, 0, 7)
    second_phase(0, 1)
    compute(1, 7, 12)
    second_phase(0, 3)
    joined(1, 2)
    joined(1, 1)
    compute(1, 12, 16)
    second_phase(0, 0)
    joined(1, 3)
    joined(1, 0)
    finish(0, 0)
    finish(0, 1)
    for p in range(2):
        sums[pl.ds(p * W, W)] = exact(lead[p], y_buf[0], (0, 0))
    early(0)
    out1[...] = -y_buf[0]
    out2[...] = exact(y_buf[0], link[...])
    second_phase(1, 2)
    early(1)
    second_phase(1, 1)
    early(2)
    second_phase(1, 3)
    early(3)
    second_phase(1, 0)
    finish(1, 0)
    finish(1, 1)
    tail[...] = exact(lead[1], y_buf[1], (0, 0))
    late(0)
    early(4)
    late(1)
    out2[...] = out2[...] - y_buf[1]
    early(5)
    late(2)
    early(6)
    diag1[...] = inv1[...] + total[pl.ds(0, W)]
    cross2[...] = jnp.transpose(total[pl.ds(W, W)]) - exact(diag1[...], link[...])
    late(3)
    diag2[...] = (inv2[...] - exact(link[...], cross2[...], (0, 0))) - exact(total[pl.ds(W, W)], link[...])
    late(4)
    late(5)
    diag2[...] = diag2[...] + last[...]

    early_swap(1 - k).wait_send()
    late_swap(1 - k).wait_send()
    for dx in (1, 2, 3):
        early_x(dx).wait_send()
        early_spread_x(dx).wait_send()
        late_x(dx).wait_send()
    for i in (4, 5):
        sent(sum_q, sum_q, i, at(dk=1)).wait_send()
    for i in (1, 5):
        late_sent(tail_q, tail_q, i, at(dk=1)).wait_send()
    early_back(k).wait_send()
    late_back(k).wait_send()
    for p in range(2):
        for q in range(4):

            @pl.when(jnp.logical_not(at_home & (x == q)))
            def _(p=p, q=q):
                quarter(p, q).wait_send()

        for way in range(2):
            for m in range(3):
                ring(p, way, m).wait_send()
        for m in range(4):
            across(p, m).wait_send()
        for h in range(2):
            for unit in UNITS:
                if roles(h, unit)[2] != "keep":
                    hop(p, h, unit).wait_send()
            for far in (1, 2, 3):
                second_send(p, h, far).wait_send()


def write_out(*refs):
    for src, dst in zip(refs[:5], refs[5:]):
        dst[...] = src[...]


def on_device(trailing, first, second, link, inv1, inv2, struct):
    f32, bf16 = jnp.float32, jnp.bfloat16
    square = jax.ShapeDtypeStruct((W, W), f32)
    tall = jax.ShapeDtypeStruct((ROWS, W), f32)
    vmem, anywhere = pl.BlockSpec(memory_space=pltpu.VMEM), pl.BlockSpec(memory_space=pl.ANY)
    dma = pltpu.SemaphoreType.DMA
    block = (ROWS, HALF)
    parts = pl.pallas_call(
        kernel,
        out_shape=(tall, square, tall, square, square),
        in_specs=[pl.BlockSpec(memory_space=pltpu.SMEM)] + [anywhere] * 6,
        out_specs=(vmem,) * 5,
        scratch_shapes=[
            pltpu.VMEM((16, ROWS, DEPTH), f32),
            pltpu.VMEM((2, 8, ROWS, W), f32),
            pltpu.VMEM((2, DEPTH, W), bf16),
            pltpu.VMEM((2, DEPTH, W), bf16),
            pltpu.VMEM((2, 16, *block), f32),
            pltpu.VMEM((2, 16, *block), f32),
            pltpu.VMEM((2, 3, 4, *block), f32),
            pltpu.VMEM((2, 3, 4, *block), f32),
            pltpu.VMEM((2, 3, *block), f32),
            pltpu.VMEM((2, 3, *block), f32),
            pltpu.VMEM((2, ROWS, W), f32),
            pltpu.VMEM((W, W), f32),
            pltpu.VMEM((W, W), f32),
            pltpu.VMEM((W, W), f32),
            pltpu.VMEM((2, ROWS, W), f32),
            pltpu.VMEM((2 * W, W), f32),
            pltpu.VMEM((W, W), f32),
            pltpu.VMEM((3, 64, W), f32),
            pltpu.VMEM((15, 8, HALF), f32),
            pltpu.VMEM((2 * W, W), f32),
            pltpu.VMEM((W, W), f32),
            pltpu.VMEM((HALF, W), f32),
            pltpu.VMEM((15, 8, W), f32),
            pltpu.VMEM((4, 8, W), f32),
            pltpu.VMEM((W, W), f32),
            dma((16,)), dma((5,)), dma((2, 4)), dma((2, 4)), dma((2, 2, 3)), dma((2, 2, 3)), dma((2, 4)), dma((2, 4)),
            dma((2, 2, 3, 4)), dma((2, 2, 3, 4)), dma((2, 2, 3)), dma((2, 2, 3)), dma((10,)), dma((10,)), dma((7,)), dma((7,)),
        ],
        compiler_params=pltpu.CompilerParams(
            collective_id=0, has_side_effects=True, vmem_limit_bytes=60 * 1024 * 1024
        ),
        name="selected_inversion",
    )(struct, trailing, first, second, link, inv1, inv2)
    return pl.pallas_call(
        write_out, out_shape=(tall, square, tall, square, square), in_specs=[vmem] * 5, out_specs=(vmem,) * 5,
        name="write_out",
    )(*parts)


def solution(mesh):
    finer = Mesh(mesh.devices.reshape(4, 2, 4, 4), AXES)
    row, col = ("x", "core"), ("z", "y")
    both = (*row, *col)
    in_specs = (P(row, col), P(both, None), P(both, None), P(), P(), P(), P())
    out_specs = (P(both, None), P(), P(both, None), P(), P())
    return jax.shard_map(on_device, mesh=finer, in_specs=in_specs, out_specs=out_specs, check_vma=False)
```

```python
import jax
import jax.numpy as jnp
from jax import lax
from jax.experimental import pallas as pl
from jax.experimental.pallas import tpu as pltpu
from jax.sharding import Mesh
from jax.sharding import PartitionSpec as P

AXES = ("x", "core", "z", "y")
MESH = pl.DeviceIdType.MESH
ROWS = 192
W = 256
HALF = 128
DEPTH = 1536

UNITS = (
    [(2, 2), (2, 3), (3, 2), (2, 1), (1, 2), (2, 0), (0, 2)]
    + [(1, 3), (3, 1), (3, 3), (1, 0), (0, 1)]
    + [(1, 1), (3, 0), (0, 3), (0, 0)]
)
PLACE = {unit: i for i, unit in enumerate(UNITS)}


def route(near, far):
    if near == 0:
        return "keep", 0
    if near == 2:
        return "relay", 1 if far % 2 == 0 else -1
    if near == 1:
        return ("joined" if far % 2 == 0 else "own"), 1
    return ("joined" if far % 2 == 1 else "own"), -1


def split(value):
    high = value.astype(jnp.bfloat16)
    return high, (value - high.astype(jnp.float32)).astype(jnp.bfloat16)


def dot(left, right):
    return jnp.dot(left, right, preferred_element_type=jnp.float32)


def exact(left, right, contract=(1, 0)):
    return lax.dot_general(
        left,
        right,
        (((contract[0],), (contract[1],)), ((), ())),
        precision=lax.Precision.HIGHEST,
        preferred_element_type=jnp.float32,
    )


def kernel(
    struct, trailing, first, second, link_in, inv1_in, inv2_in,
    out1, diag1, out2, cross2, diag2,
    t_buf, raw, lead_h, lead_l, prod_a, prod_b, got_a, got_b, far_a, far_b,
    lead, link, inv1, inv2, y_buf,
    sums, sum_p, sum_x, sum_q, total, tail, tail_p, tail_q, tail_x, last, tall, square,
    t_sem, in_sem, g1_send, g1_recv, g2_send, g2_recv, g3_send, g3_recv,
    r_send, r_recv, f_send, f_recv, s_send, s_recv, e_send, e_recv, out_sem,
):
    x, k, z, y = (lax.axis_index(name) for name in AXES)
    c = z * 4 + y
    flat = (x * 2 + k) * 16 + c
    panels = (first, second)

    def at(dx=0, dk=0, dz=0, dy=0):
        return (
            lax.rem(x + dx + 4, 4) if dx else x,
            1 - k if dk else k,
            lax.rem(z + dz + 4, 4) if dz else z,
            lax.rem(y + dy + 4, 4) if dy else y,
        )

    def remote(src, dst, send, recv, where):
        return pltpu.make_async_remote_copy(
            src_ref=src, dst_ref=dst, send_sem=send, recv_sem=recv, device_id=where, device_id_type=MESH
        )

    def t_copy(u, start=None):
        dy, dz = UNITS[u]
        block = lax.rem(z + dz, 4) * 4 + lax.rem(y + dy, 4)
        return pltpu.make_async_copy(
            trailing.at[pl.ds(pl.multiple_of(block * ROWS, ROWS), ROWS)], t_buf.at[u], t_sem.at[u]
        )

    own_copies = [
        pltpu.make_async_copy(first, lead.at[0], in_sem.at[0]),
        pltpu.make_async_copy(second, lead.at[1], in_sem.at[1]),
        pltpu.make_async_copy(link_in, link, in_sem.at[2]),
        pltpu.make_async_copy(inv1_in, inv1, in_sem.at[3]),
        pltpu.make_async_copy(inv2_in, inv2, in_sem.at[4]),
    ]
    for copy in own_copies:
        copy.start()
    for u in range(16):
        t_copy(u).start()

    target = [(q, lax.rem(z, 2), x, 2 * k + lax.div(z, 2)) for q in range(4)]
    source = [(z, lax.div(y, 2), 2 * lax.rem(y, 2) + k, i) for i in range(4)]
    at_home = (z == x) & (k == lax.rem(z, 2)) & (y == 2 * k + lax.div(z, 2))
    plane = [(o // 4, o % 4) for o in range(1, 16)]
    barrier = pltpu.get_barrier_semaphore()

    def greet(where):
        pl.semaphore_signal(barrier, inc=1, device_id=where, device_id_type=MESH)

    mate = at(dk=1)
    for i in range(4):
        for where, same in ((target[i], at_home & (x == i)), (source[i], at_home & (y == i))):
            greet(tuple(jnp.where(same, there, here) for there, here in zip(mate, where)))
    for dx in (1, 2, 3):
        greet(at(dx=dx))
    greet(at(dk=1))
    for dz, dy in plane:
        greet(at(dz=dz, dy=dy))
    mate_home = (z == x) & (1 - k == lax.rem(z, 2)) & (y == 2 * (1 - k) + lax.div(z, 2))
    pl.semaphore_wait(barrier, 27 + 2 * mate_home.astype(jnp.int32) - 2 * at_home.astype(jnp.int32))

    def quarter(p, q):
        slot = raw.at[p, lax.rem(z, 2) * 4 + y, pl.ds(q * 48, 48)]
        return remote(panels[p].at[pl.ds(q * 48, 48)], slot, g1_send.at[p], g1_recv.at[p, y], target[q])

    def quarter_home(p, q):
        slot = raw.at[p, lax.rem(z, 2) * 4 + y, pl.ds(q * 48, 48)]
        return pltpu.make_async_copy(panels[p].at[pl.ds(q * 48, 48)], slot, g1_recv.at[p, y])

    def gather_0(p):
        for q in range(4):
            same = at_home & (x == q)

            @pl.when(same)
            def _(p=p, q=q):
                quarter_home(p, q).start()

            @pl.when(jnp.logical_not(same))
            def _(p=p, q=q):
                quarter(p, q).start()

    gather_0(0)
    for copy in own_copies:
        copy.wait()
    for p in range(2):
        for s in range(3):
            rows = pl.ds(64 * s, 64)
            mask = struct[p, lax.div(flat * 3 + s, 2)].astype(jnp.float32)
            lead[p, rows] = lead[p, rows] * mask

    def piece(p, d, dx):
        q, i = lax.rem(x + dx + 4, 4), lax.rem(y + d, 4)
        return raw.at[p, 4 * k + i, pl.ds(pl.multiple_of(q * 48, 48), 48)]

    passed = ((0, 3), (1, 2))

    def ring(p, way, m):
        step = 1 if way == 0 else -1
        ref = piece(p, m, 0) if m < 4 else piece(p, passed[way][m - 4], -step)
        return remote(ref, ref, g2_send.at[p], g2_recv.at[p, way, m], at(dx=step))

    def ring_wait(p, way, m):
        step = 1 if way == 0 else -1
        ref = piece(p, m, -step) if m < 4 else piece(p, passed[way][m - 4], -2 * step)
        remote(ref, ref, g2_send.at[p], g2_recv.at[p, way, m], at(dx=step)).wait_recv()

    def across(p, m):
        q = lax.rem(x + (0, -1, 1, 2)[m] + 4, 4)
        ref = raw.at[p, pl.ds(4 * k, 4), pl.ds(pl.multiple_of(q * 48, 48), 48)]
        return remote(ref, ref, g3_send.at[p], g3_recv.at[p], at(dk=1))

    def gather_1(p):
        for d in (0, 1, 3, 2):
            ref = piece(p, d, 0)
            pltpu.make_async_copy(ref, ref, g1_recv.at[p, lax.rem(y + d, 4)]).wait()
            for way in range(2):
                ring(p, way, d).start()
        across(p, 0).start()

    def gather_2(p):
        for m in range(2):
            for way in range(2):
                ring_wait(p, way, passed[way][m])
                ring(p, way, 4 + m).start()

    def gather_3(p):
        for way in range(2):
            for d in passed[1 - way]:
                ring_wait(p, way, d)
            across(p, 1 + way).start()

    def gather_4(p):
        for way in range(2):
            for m in (4, 5):
                ring_wait(p, way, m)
        across(p, 3).start()

    def gather_5(p):
        ref = raw.at[p, pl.ds(4 * (1 - k), 4)]
        remote(ref, ref, g3_send.at[p], g3_recv.at[p], at(dk=1)).wait_recv()

        @pl.loop(0, 8)
        def _(j):
            for s in range(3):
                mask = struct[p, lax.div((c * 8 + j) * 3 + s, 2)].astype(jnp.float32)
                high, low = split(raw[p, j, pl.ds(64 * s, 64)] * mask)
                rows = pl.ds(pl.multiple_of(j * ROWS + 64 * s, 64), 64)
                lead_h[p, rows] = high
                lead_l[p, rows] = low

    def pick(h):
        return (prod_a, got_a, far_a) if h == 0 else (prod_b, got_b, far_b)

    def roles(h, unit):
        dy, dz = unit
        near, far = (dy, dz) if h == 0 else (dz, dy)
        return near, far, *route(near, far)

    def next_to(h, way, phase=1):
        along_y = (h == 0) == (phase == 1)
        return at(dy=way) if along_y else at(dz=way)

    def hop(p, h, unit):
        near, far, kind, way = roles(h, unit)
        prod, got, _ = pick(h)
        slot = 0 if kind == "relay" else (1 if way == 1 else 2)
        return remote(
            prod.at[p, PLACE[unit]], got.at[p, slot, far], r_send.at[p, h], r_recv.at[p, h, slot, far],
            next_to(h, way),
        )

    def hop_wait(p, h, slot, far):
        _, got, _ = pick(h)
        ref = got.at[p, slot, far]
        remote(ref, ref, r_send.at[p, h], r_recv.at[p, h, slot, far], next_to(h, 1)).wait_recv()

    def unit_of(h, near, far):
        return (near, far) if h == 0 else (far, near)

    def compute(p, lo, hi):
        @pl.loop(lo, hi)
        def _(u):
            if p == 0:
                for v in range(lo, hi):

                    @pl.when(u == v)
                    def _(v=v):
                        t_copy(v).wait()

            high, low = split(t_buf[u])
            wide = (dot(high, lead_h[p]) + dot(low, lead_h[p])) + dot(high, lead_l[p])
            prod_a[p, u] = wide[:, :HALF]
            prod_b[p, u] = wide[:, HALF:]
            for v in range(lo, hi):
                sends = [h for h in range(2) if roles(h, UNITS[v])[2] in ("relay", "own")]
                if sends:

                    @pl.when(u == v)
                    def _(v=v, sends=sends):
                        for h in sends:
                            hop(p, h, UNITS[v]).start()

    def joined(p, far):
        for h in range(2):
            prod, got, _ = pick(h)
            unit = unit_of(h, 1 if far % 2 == 0 else 3, far)
            hop_wait(p, h, 0, far)
            prod[p, PLACE[unit]] = prod[p, PLACE[unit]] + got[p, 0, far]
            hop(p, h, unit).start()

    def second_send(p, h, m):
        prod, _, got = pick(h)
        far, way, lo, n = ((2, 1, 0, 96), (2, -1, 96, 96), (1, 1, 0, ROWS), (3, -1, 0, ROWS))[m]
        part = pl.ds(lo, n)
        return remote(
            prod.at[p, PLACE[unit_of(h, 0, far)], part], got.at[p, max(0, m - 1), part], f_send.at[p, h],
            f_recv.at[p, h, m], next_to(h, way, phase=2),
        )

    def second_wait(p, h, m):
        _, _, got = pick(h)
        ref = got.at[p, max(0, m - 1), pl.ds(96 if m == 1 else 0, 96 if m < 2 else ROWS)]
        remote(ref, ref, f_send.at[p, h], f_recv.at[p, h, m], next_to(h, 1, phase=2)).wait_recv()

    def second_phase(p, far):
        for h in range(2):
            prod, got, last_got = pick(h)
            u = PLACE[unit_of(h, 0, far)]
            hop_wait(p, h, 1, far)
            hop_wait(p, h, 2, far)
            prod[p, u] = prod[p, u] + (got[p, 1, far] + got[p, 2, far])
            if far == 2:
                second_send(p, h, 0).start()
                second_send(p, h, 1).start()
            if far in (1, 3):
                m = far // 2
                second_wait(p, h, m)
                part = pl.ds(96 * m, 96)
                prod[p, u, part] = prod[p, u, part] + last_got[p, 0, part]
                second_send(p, h, 2 + m).start()

    def finish(p, h):
        prod, _, got = pick(h)
        second_wait(p, h, 2)
        second_wait(p, h, 3)
        value = prod[p, PLACE[(0, 0)]] + (got[p, 1] + got[p, 2])
        y_buf[p, :, pl.ds(h * HALF, HALF)] = value

    def rows(ref, start, size):
        return ref.at[pl.ds(pl.multiple_of(start, 8), size)]

    def sent(src, dst, i, where):
        return remote(src, dst, s_send.at[i], s_recv.at[i], where)

    def spot(ref, start, place):
        row = pl.multiple_of(start + 8 * lax.div(place, 2), 8)
        return ref.at[pl.ds(row, 8), pl.ds(pl.multiple_of(lax.rem(place, 2) * HALF, HALF), HALF)]

    quart = k * W + x * 64

    def early_swap(core):
        return sent(rows(sums, core * W, W), sum_p, 0, at(dk=1))

    def early_x(dx):
        there = lax.rem(x + dx, 4)
        return sent(rows(sums, k * W + there * 64, 64), sum_x.at[dx - 1], 1, at(dx=dx))

    def early_plane(o):
        dz, dy = plane[o]
        where = at(dz=dz, dy=dy)
        return sent(spot(sums, quart, where[2] * 4 + where[3]), sum_q.at[o], 2, where)

    def early_spread(o):
        dz, dy = plane[o]
        mine = spot(total, quart, c)
        return sent(mine, mine, 3, at(dz=dz, dy=dy))

    def early_spread_x(dx):
        mine = rows(total, quart, 64)
        return sent(mine, mine, 4, at(dx=dx))

    def early_back(core):
        half = rows(total, core * W, W)
        return sent(half, half, 5, at(dk=1))

    def early(step):
        if step == 0:
            early_swap(1 - k).start()
        if step == 1:
            early_swap(1 - k).wait_recv()
            half = rows(sums, k * W, W)
            half[...] = half[...] + sum_p[...]
            for dx in (2, 1, 3):
                early_x(dx).start()
        if step == 2:
            sent(sum_x, sum_x, 1, at(dk=1)).wait_recv()
            mine = rows(sums, quart, 64)
            mine[...] = (mine[...] + sum_x[0]) + (sum_x[1] + sum_x[2])
            for o in range(15):
                early_plane(o).start()
        if step == 3:
            sent(sum_q, sum_q, 2, at(dk=1)).wait_recv()
            value = spot(sums, quart, c)[...]
            for o in range(15):
                value = value + sum_q[o]
            spot(total, quart, c)[...] = value
            for o in range(15):
                early_spread(o).start()
        if step == 4:
            sent(sum_q, sum_q, 3, at(dk=1)).wait_recv()
            for dx in (2, 1, 3):
                early_spread_x(dx).start()
        if step == 5:
            sent(sum_x, sum_x, 4, at(dk=1)).wait_recv()
            early_back(k).start()
        if step == 6:
            early_back(1 - k).wait_recv()

    def late_sent(src, dst, i, where):
        return remote(src, dst, e_send.at[i], e_recv.at[i], where)

    def late_swap(core):
        return late_sent(rows(tail, core * HALF, HALF), tail_p, 0, at(dk=1))

    def late_plane(o):
        dz, dy = plane[o]
        where = at(dz=dz, dy=dy)
        return late_sent(rows(tail, k * HALF + 8 * (where[2] * 4 + where[3]), 8), tail_q.at[o], 1, where)

    def late_x(dx):
        return late_sent(tail_x.at[x], tail_x.at[x], 2, at(dx=dx))

    def late_spread(o):
        dz, dy = plane[o]
        mine = rows(last, k * HALF + 8 * c, 8)
        return late_sent(mine, mine, 3, at(dz=dz, dy=dy))

    def late_back(core):
        half = rows(last, core * HALF, HALF)
        return late_sent(half, half, 4, at(dk=1))

    def tail_half(core):
        side = lead[1, :, pl.ds(pl.multiple_of(core * HALF, HALF), HALF)]
        rows(tail, core * HALF, HALF)[...] = exact(side, y_buf[1], (0, 0))

    def late(step):
        if step == 0:
            late_swap(1 - k).start()
        if step == 1:
            late_swap(1 - k).wait_recv()
            half = rows(tail, k * HALF, HALF)
            half[...] = half[...] + tail_p[...]
            for o in range(15):
                late_plane(o).start()
        if step == 2:
            late_sent(tail_q, tail_q, 1, at(dk=1)).wait_recv()
            value = rows(tail, k * HALF + 8 * c, 8)[...]
            for o in range(15):
                value = value + tail_q[o]
            tail_x[x] = value
            for dx in (2, 1, 3):
                late_x(dx).start()
        if step == 3:
            three = tail_x.at[pl.ds(0, 3)]
            late_sent(three, three, 2, at(dx=1)).wait_recv()
            rows(last, k * HALF + 8 * c, 8)[...] = (tail_x[0] + tail_x[1]) + (tail_x[2] + tail_x[3])
            for o in range(15):
                late_spread(o).start()
        if step == 4:
            late_sent(tail_q, tail_q, 3, at(dk=1)).wait_recv()
            late_back(k).start()
        if step == 5:
            late_back(1 - k).wait_recv()

    def out_copy(i):
        src = (tall.at[0], square.at[0], tall.at[1], square.at[1], square.at[2])[i]
        dst = (out1, diag1, out2, cross2, diag2)[i]
        return pltpu.make_async_copy(src, dst, out_sem.at[i])

    gather_1(0)
    gather_2(0)
    gather_0(1)
    gather_3(0)
    gather_4(0)
    gather_5(0)
    compute(0, 0, 4)
    gather_1(1)
    compute(0, 4, 7)
    compute(0, 7, 12)
    joined(0, 2)
    gather_2(1)
    compute(0, 12, 16)
    joined(0, 3)
    joined(0, 1)
    joined(0, 0)
    gather_3(1)
    gather_4(1)
    gather_5(1)
    compute(1, 0, 4)
    second_phase(0, 2)
    compute(1, 4, 7)
    compute(1, 7, 12)
    joined(1, 2)
    compute(1, 12, 16)
    joined(1, 3)
    second_phase(0, 3)
    second_phase(0, 1)
    second_phase(0, 0)
    joined(1, 1)
    joined(1, 0)
    second_phase(1, 2)
    finish(0, 0)
    finish(0, 1)
    for p in range(2):
        sums[pl.ds(p * W, W)] = exact(lead[p], y_buf[0], (0, 0))
    early(0)
    tall[0] = -y_buf[0]
    out_copy(0).start()
    early(1)
    second_phase(1, 3)
    second_phase(1, 1)
    tall[1] = exact(y_buf[0], link[...])
    second_phase(1, 0)
    early(2)
    finish(1, 0)
    finish(1, 1)
    tail_half(1 - k)
    late(0)
    tail_half(k)
    tall[1] = tall[1] - y_buf[1]
    out_copy(2).start()
    late(1)
    early(3)
    late(2)
    early(4)
    late(3)
    early(5)
    early(6)
    square[0] = inv1[...] + total[pl.ds(0, W)]
    out_copy(1).start()
    square[1] = jnp.transpose(total[pl.ds(W, W)]) - exact(square[0], link[...])
    out_copy(3).start()
    square[2] = (inv2[...] - exact(link[...], square[1], (0, 0))) - exact(total[pl.ds(W, W)], link[...])
    for p in range(2):

        @pl.when(at_home)
        def _(p=p):
            three = raw.at[p, 0, pl.ds(0, 144)]
            remote(three, three, g1_send.at[p], g1_recv.at[p, 0], at(dk=1)).wait_send()

        @pl.when(jnp.logical_not(at_home))
        def _(p=p):
            remote(raw.at[p, 0], raw.at[p, 0], g1_send.at[p], g1_recv.at[p, 0], at(dk=1)).wait_send()

        twelve, sixteen = raw.at[p, pl.ds(0, 3)], raw.at[p, pl.ds(0, 4)]
        remote(twelve, twelve, g2_send.at[p], g2_recv.at[p, 0, 0], at(dk=1)).wait_send()
        remote(sixteen, sixteen, g3_send.at[p], g3_recv.at[p], at(dk=1)).wait_send()
        for h in range(2):
            _, got, final = pick(h)
            remote(got.at[p], got.at[p], r_send.at[p, h], r_recv.at[p, h, 0, 0], at(dk=1)).wait_send()
            remote(final.at[p], final.at[p], f_send.at[p, h], f_recv.at[p, h, 0], at(dk=1)).wait_send()
    for ref, i in ((sum_p, 0), (sum_x, 1), (sum_q, 2), (sum_q, 3), (sum_x, 4), (sum_p, 5)):
        sent(ref, ref, i, at(dk=1)).wait_send()
    for ref, i in ((tail_p, 0), (tail_q, 1), (tail_x.at[pl.ds(0, 3)], 2)):
        late_sent(ref, ref, i, at(dk=1)).wait_send()
    for i in range(4):
        out_copy(i).wait()
    late(4)
    late(5)
    square[2] = square[2] + last[...]
    out_copy(4).start()
    late_sent(tail_q, tail_q, 3, at(dk=1)).wait_send()
    late_back(k).wait_send()
    out_copy(4).wait()


def write_out(*refs):
    sources, results, held, sems = refs[:5], refs[5:10], refs[10:15], refs[15]
    into = [pltpu.make_async_copy(a, b, sems.at[0, i]) for i, (a, b) in enumerate(zip(sources, held))]
    out = [pltpu.make_async_copy(a, b, sems.at[1, i]) for i, (a, b) in enumerate(zip(held, results))]
    for copy in into:
        copy.start()
    for first, second in zip(into, out):
        first.wait()
        second.start()
    for copy in out:
        copy.wait()


def on_device(trailing, first, second, link, inv1, inv2, struct):
    f32, bf16 = jnp.float32, jnp.bfloat16
    square = jax.ShapeDtypeStruct((W, W), f32)
    tall = jax.ShapeDtypeStruct((ROWS, W), f32)
    anywhere = pl.BlockSpec(memory_space=pl.ANY)
    dma = pltpu.SemaphoreType.DMA
    block = (ROWS, HALF)
    parts = pl.pallas_call(
        kernel,
        out_shape=(tall, square, tall, square, square),
        in_specs=[pl.BlockSpec(memory_space=pltpu.SMEM)] + [anywhere] * 6,
        out_specs=(anywhere,) * 5,
        scratch_shapes=[
            pltpu.VMEM((16, ROWS, DEPTH), f32),
            pltpu.VMEM((2, 8, ROWS, W), f32),
            pltpu.VMEM((2, DEPTH, W), bf16),
            pltpu.VMEM((2, DEPTH, W), bf16),
            pltpu.VMEM((2, 16, *block), f32),
            pltpu.VMEM((2, 16, *block), f32),
            pltpu.VMEM((2, 3, 4, *block), f32),
            pltpu.VMEM((2, 3, 4, *block), f32),
            pltpu.VMEM((2, 3, *block), f32),
            pltpu.VMEM((2, 3, *block), f32),
            pltpu.VMEM((2, ROWS, W), f32),
            pltpu.VMEM((W, W), f32),
            pltpu.VMEM((W, W), f32),
            pltpu.VMEM((W, W), f32),
            pltpu.VMEM((2, ROWS, W), f32),
            pltpu.VMEM((2 * W, W), f32),
            pltpu.VMEM((W, W), f32),
            pltpu.VMEM((3, 64, W), f32),
            pltpu.VMEM((15, 8, HALF), f32),
            pltpu.VMEM((2 * W, W), f32),
            pltpu.VMEM((W, W), f32),
            pltpu.VMEM((HALF, W), f32),
            pltpu.VMEM((15, 8, W), f32),
            pltpu.VMEM((4, 8, W), f32),
            pltpu.VMEM((W, W), f32),
            pltpu.VMEM((2, ROWS, W), f32),
            pltpu.VMEM((3, W, W), f32),
            dma((16,)), dma((5,)), dma((2,)), dma((2, 4)), dma((2,)), dma((2, 2, 6)), dma((2,)), dma((2,)),
            dma((2, 2)), dma((2, 2, 3, 4)), dma((2, 2)), dma((2, 2, 4)), dma((6,)), dma((6,)), dma((5,)), dma((5,)),
            dma((5,)),
        ],
        compiler_params=pltpu.CompilerParams(
            collective_id=0, has_side_effects=True, vmem_limit_bytes=60 * 1024 * 1024
        ),
        name="selected_inversion",
    )(struct, trailing, first, second, link, inv1, inv2)
    return pl.pallas_call(
        write_out,
        out_shape=(tall, square, tall, square, square),
        in_specs=[anywhere] * 5,
        out_specs=(anywhere,) * 5,
        scratch_shapes=[pltpu.VMEM(a.shape, f32) for a in (tall, square, tall, square, square)] + [dma((2, 5))],
        compiler_params=pltpu.CompilerParams(vmem_limit_bytes=60 * 1024 * 1024),
        name="write_out",
    )(*parts)


def solution(mesh):
    finer = Mesh(mesh.devices.reshape(4, 2, 4, 4), AXES)
    row, col = ("x", "core"), ("z", "y")
    both = (*row, *col)
    in_specs = (P(row, col), P(both, None), P(both, None), P(), P(), P(), P())
    out_specs = (P(both, None), P(), P(both, None), P(), P())
    return jax.shard_map(on_device, mesh=finer, in_specs=in_specs, out_specs=out_specs, check_vma=False)
```

```python
import jax
import jax.numpy as jnp
from jax import lax
from jax.experimental import pallas as pl
from jax.experimental.pallas import tpu as pltpu
from jax.sharding import Mesh
from jax.sharding import PartitionSpec as P

AXES = ("x", "core", "z", "y")
MESH = pl.DeviceIdType.MESH
ROWS = 192
W = 256
HALF = 128
DEPTH = 1536

UNITS = (
    [(2, 2), (2, 3), (3, 2), (2, 1), (1, 2), (2, 0), (0, 2)]
    + [(1, 3), (3, 1), (3, 3), (1, 0), (0, 1)]
    + [(1, 1), (3, 0), (0, 3), (0, 0)]
)
PLACE = {unit: i for i, unit in enumerate(UNITS)}


def route(near, far):
    if near == 0:
        return "keep", 0
    if near == 2:
        return "relay", 1 if far % 2 == 0 else -1
    if near == 1:
        return ("joined" if far % 2 == 0 else "own"), 1
    return ("joined" if far % 2 == 1 else "own"), -1


def split(value):
    high = value.astype(jnp.bfloat16)
    return high, (value - high.astype(jnp.float32)).astype(jnp.bfloat16)


def dot(left, right):
    return jnp.dot(left, right, preferred_element_type=jnp.float32)


def three(left, right):
    return (dot(left[0], right[0]) + dot(left[1], right[0])) + dot(left[0], right[1])


def exact(left, right, contract=(1, 0)):
    return lax.dot_general(
        left,
        right,
        (((contract[0],), (contract[1],)), ((), ())),
        precision=lax.Precision.HIGHEST,
        preferred_element_type=jnp.float32,
    )


def kernel(
    struct, trailing, first, second, link_in, inv1_in, inv2_in,
    out1, diag1, out2, cross2, diag2,
    t_buf, raw, lead_h, lead_l, prod_a, prod_b, got_a, got_b, far_a, far_b,
    lead, near_lead, turned_h, turned_l, link, link_h, link_l, knil_h, knil_l, inv1, inv2, y_buf,
    sums, sum_p, sum_x, sum_q, total, tail, tail_p, tail_q, tail_x, last, tall, square,
    t_sem, in_sem, g1_send, g1_recv, g2_send, g2_recv, g3_send, g3_recv,
    n_sem, r_send, r_recv, f_send, f_recv, s_send, s_recv, e_send, e_recv, out_sem,
):
    x, k, z, y = (lax.axis_index(name) for name in AXES)
    c = z * 4 + y
    flat = (x * 2 + k) * 16 + c
    panels = (first, second)

    def at(dx=0, dk=0, dz=0, dy=0):
        return (
            lax.rem(x + dx + 4, 4) if dx else x,
            1 - k if dk else k,
            lax.rem(z + dz + 4, 4) if dz else z,
            lax.rem(y + dy + 4, 4) if dy else y,
        )

    def remote(src, dst, send, recv, where):
        return pltpu.make_async_remote_copy(
            src_ref=src, dst_ref=dst, send_sem=send, recv_sem=recv, device_id=where, device_id_type=MESH
        )

    def t_copy(u, start=None):
        dy, dz = UNITS[u]
        block = lax.rem(z + dz, 4) * 4 + lax.rem(y + dy, 4)
        return pltpu.make_async_copy(
            trailing.at[pl.ds(pl.multiple_of(block * ROWS, ROWS), ROWS)], t_buf.at[u], t_sem.at[u]
        )

    own_copies = [
        pltpu.make_async_copy(first, lead.at[0], in_sem.at[0]),
        pltpu.make_async_copy(second, lead.at[1], in_sem.at[1]),
        pltpu.make_async_copy(link_in, link, in_sem.at[2]),
        pltpu.make_async_copy(inv1_in, inv1, in_sem.at[3]),
        pltpu.make_async_copy(inv2_in, inv2, in_sem.at[4]),
    ]
    for copy in own_copies:
        copy.start()
    for u in range(16):
        t_copy(u).start()

    target = [(q, lax.rem(z, 2), x, 2 * k + lax.div(z, 2)) for q in range(4)]
    source = [(z, lax.div(y, 2), 2 * lax.rem(y, 2) + k, i) for i in range(4)]
    at_home = (z == x) & (k == lax.rem(z, 2)) & (y == 2 * k + lax.div(z, 2))
    plane = [(o // 4, o % 4) for o in range(1, 16)]
    barrier = pltpu.get_barrier_semaphore()

    def greet(where):
        pl.semaphore_signal(barrier, inc=1, device_id=where, device_id_type=MESH)

    mate = at(dk=1)
    for i in range(4):
        for where, same in ((target[i], at_home & (x == i)), (source[i], at_home & (y == i))):
            greet(tuple(jnp.where(same, there, here) for there, here in zip(mate, where)))
    for dx in (1, 2, 3):
        greet(at(dx=dx))
    greet(at(dk=1))
    for dz, dy in plane:
        greet(at(dz=dz, dy=dy))
    mate_home = (z == x) & (1 - k == lax.rem(z, 2)) & (y == 2 * (1 - k) + lax.div(z, 2))
    pl.semaphore_wait(barrier, 27 + 2 * mate_home.astype(jnp.int32) - 2 * at_home.astype(jnp.int32))

    def quarter(p, q):
        slot = raw.at[p, lax.rem(z, 2) * 4 + y, pl.ds(q * 48, 48)]
        return remote(panels[p].at[pl.ds(q * 48, 48)], slot, g1_send.at[p], g1_recv.at[p, y], target[q])

    def quarter_home(p, q):
        slot = raw.at[p, lax.rem(z, 2) * 4 + y, pl.ds(q * 48, 48)]
        return pltpu.make_async_copy(panels[p].at[pl.ds(q * 48, 48)], slot, g1_recv.at[p, y])

    def gather_0(p):
        for q in range(4):
            same = at_home & (x == q)

            @pl.when(same)
            def _(p=p, q=q):
                quarter_home(p, q).start()

            @pl.when(jnp.logical_not(same))
            def _(p=p, q=q):
                quarter(p, q).start()

    gather_0(0)
    for copy in own_copies:
        copy.wait()
    for p in range(2):
        for s in range(3):
            rows = pl.ds(64 * s, 64)
            mask = struct[p, lax.div(flat * 3 + s, 2)].astype(jnp.float32)
            lead[p, rows] = lead[p, rows] * mask

    def piece(p, d, dx):
        q, i = lax.rem(x + dx + 4, 4), lax.rem(y + d, 4)
        return raw.at[p, 4 * k + i, pl.ds(pl.multiple_of(q * 48, 48), 48)]

    passed = ((0, 3), (1, 2))

    def ring(p, way, m):
        step = 1 if way == 0 else -1
        ref = piece(p, m, 0) if m < 4 else piece(p, passed[way][m - 4], -step)
        return remote(ref, ref, g2_send.at[p], g2_recv.at[p, way, m], at(dx=step))

    def ring_wait(p, way, m):
        step = 1 if way == 0 else -1
        ref = piece(p, m, -step) if m < 4 else piece(p, passed[way][m - 4], -2 * step)
        remote(ref, ref, g2_send.at[p], g2_recv.at[p, way, m], at(dx=step)).wait_recv()

    def across(p, m):
        q = lax.rem(x + (0, -1, 1, 2)[m] + 4, 4)
        ref = raw.at[p, pl.ds(4 * k, 4), pl.ds(pl.multiple_of(q * 48, 48), 48)]
        return remote(ref, ref, g3_send.at[p], g3_recv.at[p], at(dk=1))

    def gather_1(p):
        for d in (0, 1, 3, 2):
            ref = piece(p, d, 0)
            pltpu.make_async_copy(ref, ref, g1_recv.at[p, lax.rem(y + d, 4)]).wait()
            for way in range(2):
                ring(p, way, d).start()
        across(p, 0).start()

    def gather_2(p):
        for m in range(2):
            for way in range(2):
                ring_wait(p, way, passed[way][m])
                ring(p, way, 4 + m).start()

    def gather_3(p):
        for way in range(2):
            for d in passed[1 - way]:
                ring_wait(p, way, d)
            across(p, 1 + way).start()

    def gather_4(p):
        for way in range(2):
            for m in (4, 5):
                ring_wait(p, way, m)
        across(p, 3).start()

    def gather_5(p):
        ref = raw.at[p, pl.ds(4 * (1 - k), 4)]
        remote(ref, ref, g3_send.at[p], g3_recv.at[p], at(dk=1)).wait_recv()

        @pl.loop(0, 8)
        def _(j):
            for s in range(3):
                mask = struct[p, lax.div((c * 8 + j) * 3 + s, 2)].astype(jnp.float32)
                high, low = split(raw[p, j, pl.ds(64 * s, 64)] * mask)
                rows = pl.ds(pl.multiple_of(j * ROWS + 64 * s, 64), 64)
                lead_h[p, rows] = high
                lead_l[p, rows] = low

    def share(slot):
        far = slot % 3 + 1
        where = at(dz=4 - far) if slot < 3 else at(dy=4 - far)
        return remote(second, near_lead.at[slot], n_sem.at[0], n_sem.at[1], where)

    def share_done():
        remote(near_lead, near_lead, n_sem.at[0], n_sem.at[1], at(dk=1)).wait_recv()
        for slot in range(6):
            far = slot % 3 + 1
            place = lax.rem(z + far, 4) * 4 + y if slot < 3 else z * 4 + lax.rem(y + far, 4)
            for s in range(3):
                part = pl.ds(64 * s, 64)
                mask = struct[1, lax.div(((x * 2 + k) * 16 + place) * 3 + s, 2)].astype(jnp.float32)
                near_lead[slot, part] = near_lead[slot, part] * mask
        for slot in range(7):
            turned_h[slot], turned_l[slot] = split(jnp.transpose(lead[1] if slot == 6 else near_lead[slot]))
        link_h[...], link_l[...] = split(link[...])
        knil_h[...], knil_l[...] = split(jnp.transpose(link[...]))

    def pick(h):
        return (prod_a, got_a, far_a) if h == 0 else (prod_b, got_b, far_b)

    def roles(h, unit):
        dy, dz = unit
        near, far = (dy, dz) if h == 0 else (dz, dy)
        return near, far, *route(near, far)

    def next_to(h, way, phase=1):
        along_y = (h == 0) == (phase == 1)
        return at(dy=way) if along_y else at(dz=way)

    def hop(p, h, unit):
        near, far, kind, way = roles(h, unit)
        prod, got, _ = pick(h)
        slot = 0 if kind == "relay" else (1 if way == 1 else 2)
        return remote(
            prod.at[p, PLACE[unit]], got.at[p, slot, far], r_send.at[p, h], r_recv.at[p, h, slot, far],
            next_to(h, way),
        )

    def hop_wait(p, h, slot, far):
        _, got, _ = pick(h)
        ref = got.at[p, slot, far]
        remote(ref, ref, r_send.at[p, h], r_recv.at[p, h, slot, far], next_to(h, 1)).wait_recv()

    def unit_of(h, near, far):
        return (near, far) if h == 0 else (far, near)

    def compute(p, lo, hi):
        @pl.loop(lo, hi)
        def _(u):
            if p == 0:
                for v in range(lo, hi):

                    @pl.when(u == v)
                    def _(v=v):
                        t_copy(v).wait()

            high, low = split(t_buf[u])
            wide = (dot(high, lead_h[p]) + dot(low, lead_h[p])) + dot(high, lead_l[p])
            prod_a[p, u] = wide[:, :HALF]
            prod_b[p, u] = wide[:, HALF:]
            for v in range(lo, hi):
                sends = [h for h in range(2) if roles(h, UNITS[v])[2] in ("relay", "own")]
                if sends:

                    @pl.when(u == v)
                    def _(v=v, sends=sends):
                        for h in sends:
                            hop(p, h, UNITS[v]).start()

    def joined(p, far):
        for h in range(2):
            prod, got, _ = pick(h)
            unit = unit_of(h, 1 if far % 2 == 0 else 3, far)
            hop_wait(p, h, 0, far)
            prod[p, PLACE[unit]] = prod[p, PLACE[unit]] + got[p, 0, far]
            hop(p, h, unit).start()

    def second_send(p, h, m):
        prod, _, got = pick(h)
        if p == 0:
            far = m + 1
            return remote(
                prod.at[p, PLACE[unit_of(h, 0, far)]], got.at[p, m], f_send.at[p, h], f_recv.at[p, h, m],
                next_to(h, far, phase=2),
            )
        far, way, lo, n = ((2, 1, 0, 96), (2, -1, 96, 96), (1, 1, 0, ROWS), (3, -1, 0, ROWS))[m]
        part = pl.ds(lo, n)
        return remote(
            prod.at[p, PLACE[unit_of(h, 0, far)], part], got.at[p, max(0, m - 1), part], f_send.at[p, h],
            f_recv.at[p, h, m], next_to(h, way, phase=2),
        )

    def second_wait(p, h, m):
        _, _, got = pick(h)
        if p == 0:
            ref = got.at[p, m]
        else:
            ref = got.at[p, max(0, m - 1), pl.ds(96 if m == 1 else 0, 96 if m < 2 else ROWS)]
        remote(ref, ref, f_send.at[p, h], f_recv.at[p, h, m], next_to(h, 1, phase=2)).wait_recv()

    def second_phase(p, far):
        for h in range(2):
            prod, got, _ = pick(h)
            u = PLACE[unit_of(h, 0, far)]
            hop_wait(p, h, 1, far)
            hop_wait(p, h, 2, far)
            prod[p, u] = prod[p, u] + (got[p, 1, far] + got[p, 2, far])
            if p == 0 and far:
                second_send(p, h, far - 1).start()
            if p == 1 and far == 2:
                second_send(p, h, 0).start()
                second_send(p, h, 1).start()

    def gain(far):
        for h in range(2):
            prod, _, _ = pick(h)
            slot = 6 if far == 0 else far - 1 + 3 * h
            part = three((turned_h[slot], turned_l[slot]), split(prod[1, PLACE[unit_of(h, 0, far)]]))
            cols = pl.ds(h * HALF, HALF)
            tail[:, cols] = part if far == 2 else tail[:, cols] + part

    def pass_on(far):
        m = far // 2
        for h in range(2):
            prod, _, got = pick(h)
            u = PLACE[unit_of(h, 0, far)]
            second_wait(1, h, m)
            part = pl.ds(96 * m, 96)
            prod[1, u, part] = prod[1, u, part] + got[1, 0, part]
            second_send(1, h, 2 + m).start()

    def finish(p):
        for h in range(2):
            prod, _, got = pick(h)
            value = prod[p, PLACE[(0, 0)]]
            if p == 0:
                for m in range(3):
                    second_wait(p, h, m)
                value = (value + got[p, 0]) + (got[p, 1] + got[p, 2])
            else:
                second_wait(p, h, 2)
                second_wait(p, h, 3)
                value = value + (got[p, 1] + got[p, 2])
            y_buf[p, :, pl.ds(h * HALF, HALF)] = value

    def rows(ref, start, size):
        return ref.at[pl.ds(pl.multiple_of(start, 8), size)]

    def sent(src, dst, i, where):
        return remote(src, dst, s_send.at[i], s_recv.at[i], where)

    def spot(ref, start, place):
        row = pl.multiple_of(start + 8 * lax.div(place, 2), 8)
        return ref.at[pl.ds(row, 8), pl.ds(pl.multiple_of(lax.rem(place, 2) * HALF, HALF), HALF)]

    quart = k * W + x * 64

    def early_swap(core):
        return sent(rows(sums, core * W, W), sum_p, 0, at(dk=1))

    def early_x(dx):
        there = lax.rem(x + dx, 4)
        return sent(rows(sums, k * W + there * 64, 64), sum_x.at[dx - 1], 1, at(dx=dx))

    def early_plane(o):
        dz, dy = plane[o]
        where = at(dz=dz, dy=dy)
        return sent(spot(sums, quart, where[2] * 4 + where[3]), sum_q.at[o], 2, where)

    def early_spread(o):
        dz, dy = plane[o]
        mine = spot(total, quart, c)
        return sent(mine, mine, 3, at(dz=dz, dy=dy))

    def early_spread_x(dx):
        mine = rows(total, quart, 64)
        return sent(mine, mine, 4, at(dx=dx))

    def early_back(core):
        half = rows(total, core * W, W)
        return sent(half, half, 5, at(dk=1))

    def early(step):
        if step == 0:
            early_swap(1 - k).start()
        if step == 1:
            early_swap(1 - k).wait_recv()
            half = rows(sums, k * W, W)
            half[...] = half[...] + sum_p[...]
            for dx in (2, 1, 3):
                early_x(dx).start()
        if step == 2:
            sent(sum_x, sum_x, 1, at(dk=1)).wait_recv()
            mine = rows(sums, quart, 64)
            mine[...] = (mine[...] + sum_x[0]) + (sum_x[1] + sum_x[2])
            for o in range(15):
                early_plane(o).start()
        if step == 3:
            sent(sum_q, sum_q, 2, at(dk=1)).wait_recv()
            value = spot(sums, quart, c)[...]
            for o in range(15):
                value = value + sum_q[o]
            spot(total, quart, c)[...] = value
            for o in range(15):
                early_spread(o).start()
        if step == 4:
            sent(sum_q, sum_q, 3, at(dk=1)).wait_recv()
            for dx in (2, 1, 3):
                early_spread_x(dx).start()
        if step == 5:
            sent(sum_x, sum_x, 4, at(dk=1)).wait_recv()
            early_back(k).start()
        if step == 6:
            early_back(1 - k).wait_recv()

    def late_sent(src, dst, i, where):
        return remote(src, dst, e_send.at[i], e_recv.at[i], where)

    def late_swap(core):
        return late_sent(rows(tail, core * HALF, HALF), tail_p, 0, at(dk=1))

    def late_plane(o):
        dz, dy = plane[o]
        where = at(dz=dz, dy=dy)
        return late_sent(rows(tail, k * HALF + 8 * (where[2] * 4 + where[3]), 8), tail_q.at[o], 1, where)

    def late_x(dx):
        return late_sent(tail_x.at[x], tail_x.at[x], 2, at(dx=dx))

    def late_spread(o):
        dz, dy = plane[o]
        mine = rows(last, k * HALF + 8 * c, 8)
        return late_sent(mine, mine, 3, at(dz=dz, dy=dy))

    def late_back(core):
        half = rows(last, core * HALF, HALF)
        return late_sent(half, half, 4, at(dk=1))

    def late(step):
        if step == 0:
            late_swap(1 - k).start()
        if step == 1:
            late_swap(1 - k).wait_recv()
            half = rows(tail, k * HALF, HALF)
            half[...] = half[...] + tail_p[...]
            for o in range(15):
                late_plane(o).start()
        if step == 2:
            late_sent(tail_q, tail_q, 1, at(dk=1)).wait_recv()
            value = rows(tail, k * HALF + 8 * c, 8)[...]
            for o in range(15):
                value = value + tail_q[o]
            tail_x[x] = value
            for dx in (2, 1, 3):
                late_x(dx).start()
        if step == 3:
            three = tail_x.at[pl.ds(0, 3)]
            late_sent(three, three, 2, at(dx=1)).wait_recv()
            rows(last, k * HALF + 8 * c, 8)[...] = (tail_x[0] + tail_x[1]) + (tail_x[2] + tail_x[3])
            for o in range(15):
                late_spread(o).start()
        if step == 4:
            late_sent(tail_q, tail_q, 3, at(dk=1)).wait_recv()
            late_back(k).start()
        if step == 5:
            late_back(1 - k).wait_recv()

    def out_copy(i):
        src = (tall.at[0], square.at[0], tall.at[1], square.at[1], square.at[2])[i]
        dst = (out1, diag1, out2, cross2, diag2)[i]
        return pltpu.make_async_copy(src, dst, out_sem.at[i])

    gather_1(0)
    gather_0(1)
    for slot in (0, 3, 2, 5):
        share(slot).start()
    gather_2(0)
    for slot in (1, 4):
        share(slot).start()
    gather_3(0)
    gather_4(0)
    gather_5(0)
    gather_1(1)
    compute(0, 0, 4)
    compute(0, 4, 7)
    gather_2(1)
    compute(0, 7, 12)
    joined(0, 2)
    gather_3(1)
    compute(0, 12, 14)
    gather_4(1)
    compute(0, 14, 16)
    joined(0, 3)
    joined(0, 1)
    joined(0, 0)
    gather_5(1)
    compute(1, 0, 4)
    second_phase(0, 2)
    compute(1, 4, 7)
    second_phase(0, 3)
    second_phase(0, 1)
    compute(1, 7, 12)
    joined(1, 2)
    second_phase(0, 0)
    compute(1, 12, 16)
    joined(1, 3)
    joined(1, 1)
    joined(1, 0)
    finish(0)
    for p in range(2):
        sums[pl.ds(p * W, W)] = exact(lead[p], y_buf[0], (0, 0))
    early(0)
    share_done()
    early(1)
    second_phase(1, 2)
    gain(2)
    second_phase(1, 3)
    gain(3)
    second_phase(1, 1)
    gain(1)
    second_phase(1, 0)
    gain(0)
    late(0)
    tall[0] = -y_buf[0]
    out_copy(0).start()
    early(2)
    late(1)
    pass_on(3)
    pass_on(1)
    tall[1] = exact(y_buf[0], link[...])
    early(3)
    late(2)
    finish(1)
    tall[1] = tall[1] - y_buf[1]
    out_copy(2).start()
    late(3)
    early(4)
    early(5)
    late(4)
    for p in range(2):

        @pl.when(at_home)
        def _(p=p):
            three = raw.at[p, 0, pl.ds(0, 144)]
            remote(three, three, g1_send.at[p], g1_recv.at[p, 0], at(dk=1)).wait_send()

        @pl.when(jnp.logical_not(at_home))
        def _(p=p):
            remote(raw.at[p, 0], raw.at[p, 0], g1_send.at[p], g1_recv.at[p, 0], at(dk=1)).wait_send()

        twelve, sixteen = raw.at[p, pl.ds(0, 3)], raw.at[p, pl.ds(0, 4)]
        remote(twelve, twelve, g2_send.at[p], g2_recv.at[p, 0, 0], at(dk=1)).wait_send()
        remote(sixteen, sixteen, g3_send.at[p], g3_recv.at[p], at(dk=1)).wait_send()
        for h in range(2):
            _, got, final = pick(h)
            remote(got.at[p], got.at[p], r_send.at[p, h], r_recv.at[p, h, 0, 0], at(dk=1)).wait_send()
            remote(final.at[p], final.at[p], f_send.at[p, h], f_recv.at[p, h, 0], at(dk=1)).wait_send()
    for ref, i in ((sum_p, 0), (sum_x, 1), (sum_q, 2), (sum_q, 3), (sum_x, 4)):
        sent(ref, ref, i, at(dk=1)).wait_send()
    for ref, i in ((tail_p, 0), (tail_q, 1), (tail_x.at[pl.ds(0, 3)], 2)):
        late_sent(ref, ref, i, at(dk=1)).wait_send()
    late_sent(tail_q, tail_q, 3, at(dk=1)).wait_send()
    remote(near_lead, near_lead, n_sem.at[0], n_sem.at[1], at(dk=1)).wait_send()
    for i in (0, 2):
        out_copy(i).wait()
    early(6)
    square[0] = inv1[...] + total[pl.ds(0, W)]
    out_copy(1).start()
    link_parts, cross_sum = (link_h[...], link_l[...]), total[pl.ds(W, W)]
    square[1] = jnp.transpose(cross_sum) - three(split(square[0]), link_parts)
    out_copy(3).start()
    square[2] = (inv2[...] - three((knil_h[...], knil_l[...]), split(square[1]))) - three(
        split(cross_sum), link_parts
    )
    late(5)
    square[2] = square[2] + last[...]
    out_copy(4).start()
    late_back(k).wait_send()
    sent(sum_p, sum_p, 5, at(dk=1)).wait_send()
    for i in (1, 3, 4):
        out_copy(i).wait()


def write_out(*refs):
    sources, results, held, sems = refs[:5], refs[5:10], refs[10:15], refs[15]
    into = [pltpu.make_async_copy(a, b, sems.at[0, i]) for i, (a, b) in enumerate(zip(sources, held))]
    out = [pltpu.make_async_copy(a, b, sems.at[1, i]) for i, (a, b) in enumerate(zip(held, results))]
    for copy in into:
        copy.start()
    for first, second in zip(into, out):
        first.wait()
        second.start()
    for copy in out:
        copy.wait()


def on_device(trailing, first, second, link, inv1, inv2, struct):
    f32, bf16 = jnp.float32, jnp.bfloat16
    square = jax.ShapeDtypeStruct((W, W), f32)
    tall = jax.ShapeDtypeStruct((ROWS, W), f32)
    anywhere = pl.BlockSpec(memory_space=pl.ANY)
    dma = pltpu.SemaphoreType.DMA
    block = (ROWS, HALF)
    parts = pl.pallas_call(
        kernel,
        out_shape=(tall, square, tall, square, square),
        in_specs=[pl.BlockSpec(memory_space=pltpu.SMEM)] + [anywhere] * 6,
        out_specs=(anywhere,) * 5,
        scratch_shapes=[
            pltpu.VMEM((16, ROWS, DEPTH), f32),
            pltpu.VMEM((2, 8, ROWS, W), f32),
            pltpu.VMEM((2, DEPTH, W), bf16),
            pltpu.VMEM((2, DEPTH, W), bf16),
            pltpu.VMEM((2, 16, *block), f32),
            pltpu.VMEM((2, 16, *block), f32),
            pltpu.VMEM((2, 3, 4, *block), f32),
            pltpu.VMEM((2, 3, 4, *block), f32),
            pltpu.VMEM((2, 3, *block), f32),
            pltpu.VMEM((2, 3, *block), f32),
            pltpu.VMEM((2, ROWS, W), f32),
            pltpu.VMEM((6, ROWS, W), f32),
            pltpu.VMEM((7, W, ROWS), bf16),
            pltpu.VMEM((7, W, ROWS), bf16),
            pltpu.VMEM((W, W), f32),
            pltpu.VMEM((W, W), bf16),
            pltpu.VMEM((W, W), bf16),
            pltpu.VMEM((W, W), bf16),
            pltpu.VMEM((W, W), bf16),
            pltpu.VMEM((W, W), f32),
            pltpu.VMEM((W, W), f32),
            pltpu.VMEM((2, ROWS, W), f32),
            pltpu.VMEM((2 * W, W), f32),
            pltpu.VMEM((W, W), f32),
            pltpu.VMEM((3, 64, W), f32),
            pltpu.VMEM((15, 8, HALF), f32),
            pltpu.VMEM((2 * W, W), f32),
            pltpu.VMEM((W, W), f32),
            pltpu.VMEM((HALF, W), f32),
            pltpu.VMEM((15, 8, W), f32),
            pltpu.VMEM((4, 8, W), f32),
            pltpu.VMEM((W, W), f32),
            pltpu.VMEM((2, ROWS, W), f32),
            pltpu.VMEM((3, W, W), f32),
            dma((16,)), dma((5,)), dma((2,)), dma((2, 4)), dma((2,)), dma((2, 2, 6)), dma((2,)), dma((2,)),
            dma((2,)), dma((2, 2)), dma((2, 2, 3, 4)), dma((2, 2)), dma((2, 2, 4)), dma((6,)), dma((6,)), dma((5,)), dma((5,)),
            dma((5,)),
        ],
        compiler_params=pltpu.CompilerParams(
            collective_id=0, has_side_effects=True, vmem_limit_bytes=60 * 1024 * 1024
        ),
        name="selected_inversion",
    )(struct, trailing, first, second, link, inv1, inv2)
    return pl.pallas_call(
        write_out,
        out_shape=(tall, square, tall, square, square),
        in_specs=[anywhere] * 5,
        out_specs=(anywhere,) * 5,
        scratch_shapes=[pltpu.VMEM(a.shape, f32) for a in (tall, square, tall, square, square)] + [dma((2, 5))],
        compiler_params=pltpu.CompilerParams(vmem_limit_bytes=60 * 1024 * 1024),
        name="write_out",
    )(*parts)


def solution(mesh):
    finer = Mesh(mesh.devices.reshape(4, 2, 4, 4), AXES)
    row, col = ("x", "core"), ("z", "y")
    both = (*row, *col)
    in_specs = (P(row, col), P(both, None), P(both, None), P(), P(), P(), P())
    out_specs = (P(both, None), P(), P(both, None), P(), P())
    return jax.shard_map(on_device, mesh=finer, in_specs=in_specs, out_specs=out_specs, check_vma=False)
```

```python
import jax
import jax.numpy as jnp
from jax import lax
from jax.experimental import pallas as pl
from jax.experimental.pallas import tpu as pltpu
from jax.sharding import Mesh
from jax.sharding import PartitionSpec as P

AXES = ("x", "core", "z", "y")
MESH = pl.DeviceIdType.MESH
ROWS = 192
W = 256
HALF = 128
DEPTH = 1536

UNITS = (
    [(2, 2), (2, 3), (3, 2), (2, 1), (1, 2), (2, 0), (0, 2)]
    + [(1, 3), (3, 1), (3, 3), (1, 0), (0, 1)]
    + [(1, 1), (3, 0), (0, 3), (0, 0)]
)
PLACE = {unit: i for i, unit in enumerate(UNITS)}


def route(near, far):
    if near == 0:
        return "keep", 0
    if near == 2:
        return "relay", 1 if far % 2 == 0 else -1
    if near == 1:
        return ("joined" if far % 2 == 0 else "own"), 1
    return ("joined" if far % 2 == 1 else "own"), -1


def split(value):
    high = value.astype(jnp.bfloat16)
    return high, (value - high.astype(jnp.float32)).astype(jnp.bfloat16)


def dot(left, right):
    return jnp.dot(left, right, preferred_element_type=jnp.float32)


def three(left, right):
    return (dot(left[0], right[0]) + dot(left[1], right[0])) + dot(left[0], right[1])


def exact(left, right, contract=(1, 0)):
    return lax.dot_general(
        left,
        right,
        (((contract[0],), (contract[1],)), ((), ())),
        precision=lax.Precision.HIGHEST,
        preferred_element_type=jnp.float32,
    )


def kernel(
    struct, trailing, first, second, link_in, inv1_in, inv2_in,
    out1, diag1, out2, cross2, diag2,
    t_buf, raw, lead_h, lead_l, prod_a, prod_b, got_a, got_b, far_a, far_b,
    lead, near_lead, turned_h, turned_l, link, link_h, link_l, knil_h, knil_l, inv1, inv2, y_buf,
    sums, sum_p, sum_x, sum_q, total, tail, tail_p, tail_q, tail_x, last, tall, square,
    t_sem, in_sem, g1_send, g1_recv, g2_send, g2_recv, g3_send, g3_recv,
    n_sem, r_send, r_recv, f_send, f_recv, s_send, s_recv, e_send, e_recv, out_sem,
):
    x, k, z, y = (lax.axis_index(name) for name in AXES)
    c = z * 4 + y
    flat = (x * 2 + k) * 16 + c
    panels = (first, second)

    def at(dx=0, dk=0, dz=0, dy=0):
        return (
            lax.rem(x + dx + 4, 4) if dx else x,
            1 - k if dk else k,
            lax.rem(z + dz + 4, 4) if dz else z,
            lax.rem(y + dy + 4, 4) if dy else y,
        )

    def remote(src, dst, send, recv, where):
        return pltpu.make_async_remote_copy(
            src_ref=src, dst_ref=dst, send_sem=send, recv_sem=recv, device_id=where, device_id_type=MESH
        )

    def t_copy(u, start=None):
        dy, dz = UNITS[u]
        block = lax.rem(z + dz, 4) * 4 + lax.rem(y + dy, 4)
        return pltpu.make_async_copy(
            trailing.at[pl.ds(pl.multiple_of(block * ROWS, ROWS), ROWS)], t_buf.at[u], t_sem.at[u]
        )

    own_copies = [
        pltpu.make_async_copy(first, lead.at[0], in_sem.at[0]),
        pltpu.make_async_copy(second, lead.at[1], in_sem.at[1]),
        pltpu.make_async_copy(link_in, link, in_sem.at[2]),
        pltpu.make_async_copy(inv1_in, inv1, in_sem.at[3]),
        pltpu.make_async_copy(inv2_in, inv2, in_sem.at[4]),
    ]
    for copy in own_copies:
        copy.start()
    for u in range(16):
        t_copy(u).start()

    target = [(q, lax.rem(z, 2), x, 2 * k + lax.div(z, 2)) for q in range(4)]
    source = [(z, lax.div(y, 2), 2 * lax.rem(y, 2) + k, i) for i in range(4)]
    at_home = (z == x) & (k == lax.rem(z, 2)) & (y == 2 * k + lax.div(z, 2))
    plane = [(o // 4, o % 4) for o in range(1, 16)]
    barrier = pltpu.get_barrier_semaphore()

    def greet(where):
        pl.semaphore_signal(barrier, inc=1, device_id=where, device_id_type=MESH)

    mate = at(dk=1)
    for i in range(4):
        for where, same in ((target[i], at_home & (x == i)), (source[i], at_home & (y == i))):
            greet(tuple(jnp.where(same, there, here) for there, here in zip(mate, where)))
    for dx in (1, 2, 3):
        greet(at(dx=dx))
    greet(at(dk=1))
    for dz, dy in plane:
        greet(at(dz=dz, dy=dy))
    mate_home = (z == x) & (1 - k == lax.rem(z, 2)) & (y == 2 * (1 - k) + lax.div(z, 2))
    pl.semaphore_wait(barrier, 27 + 2 * mate_home.astype(jnp.int32) - 2 * at_home.astype(jnp.int32))

    def quarter(p, q):
        slot = raw.at[p, lax.rem(z, 2) * 4 + y, pl.ds(q * 48, 48)]
        return remote(panels[p].at[pl.ds(q * 48, 48)], slot, g1_send.at[p], g1_recv.at[p, y], target[q])

    def quarter_home(p, q):
        slot = raw.at[p, lax.rem(z, 2) * 4 + y, pl.ds(q * 48, 48)]
        return pltpu.make_async_copy(panels[p].at[pl.ds(q * 48, 48)], slot, g1_recv.at[p, y])

    def gather_0(p):
        for q in range(4):
            same = at_home & (x == q)

            @pl.when(same)
            def _(p=p, q=q):
                quarter_home(p, q).start()

            @pl.when(jnp.logical_not(same))
            def _(p=p, q=q):
                quarter(p, q).start()

    gather_0(0)
    for copy in own_copies:
        copy.wait()
    for p in range(2):
        for s in range(3):
            rows = pl.ds(64 * s, 64)
            mask = struct[p, lax.div(flat * 3 + s, 2)].astype(jnp.float32)
            lead[p, rows] = lead[p, rows] * mask

    def piece(p, d, dx):
        q, i = lax.rem(x + dx + 4, 4), lax.rem(y + d, 4)
        return raw.at[p, 4 * k + i, pl.ds(pl.multiple_of(q * 48, 48), 48)]

    passed = ((0, 3), (1, 2))

    def ring_sem(way, m):
        return 3 if m > 3 else (passed[way].index(m) if m in passed[way] else 2)

    def ring(p, way, m):
        step = 1 if way == 0 else -1
        ref = piece(p, m, 0) if m < 4 else piece(p, passed[way][m - 4], -step)
        return remote(ref, ref, g2_send.at[p], g2_recv.at[p, way, ring_sem(way, m)], at(dx=step))

    def ring_wait(p, way, i):
        ref = raw.at[p, 0, pl.ds(0, 48 if i < 2 else 96)]
        remote(ref, ref, g2_send.at[p], g2_recv.at[p, way, i], at(dk=1)).wait_recv()

    def across(p, m):
        q = lax.rem(x + (0, -1, 1, 2)[m] + 4, 4)
        ref = raw.at[p, pl.ds(4 * k, 4), pl.ds(pl.multiple_of(q * 48, 48), 48)]
        return remote(ref, ref, g3_send.at[p], g3_recv.at[p], at(dk=1))

    def gather_1(p):
        for d in (0, 1, 3, 2):
            ref = piece(p, d, 0)
            pltpu.make_async_copy(ref, ref, g1_recv.at[p, lax.rem(y + d, 4)]).wait()
            for way in range(2):
                ring(p, way, d).start()
        across(p, 0).start()

    def gather_2(p):
        for m in range(2):
            for way in range(2):
                ring_wait(p, way, m)
                ring(p, way, 4 + m).start()

    def gather_3(p):
        for way in range(2):
            ring_wait(p, way, 2)
            across(p, 1 + way).start()

    def gather_4(p):
        for way in range(2):
            ring_wait(p, way, 3)
        across(p, 3).start()

    def gather_5(p):
        ref = raw.at[p, pl.ds(4 * (1 - k), 4)]
        remote(ref, ref, g3_send.at[p], g3_recv.at[p], at(dk=1)).wait_recv()

        @pl.loop(0, 8)
        def _(j):
            for s in range(3):
                mask = struct[p, lax.div((c * 8 + j) * 3 + s, 2)].astype(jnp.float32)
                high, low = split(raw[p, j, pl.ds(64 * s, 64)] * mask)
                rows = pl.ds(pl.multiple_of(j * ROWS + 64 * s, 64), 64)
                lead_h[p, rows] = high
                lead_l[p, rows] = low

    def share(slot):
        far = slot % 3 + 1
        where = at(dz=4 - far) if slot < 3 else at(dy=4 - far)
        return remote(second, near_lead.at[slot], n_sem.at[0], n_sem.at[1], where)

    def share_done():
        remote(near_lead, near_lead, n_sem.at[0], n_sem.at[1], at(dk=1)).wait_recv()
        for slot in range(6):
            far = slot % 3 + 1
            place = lax.rem(z + far, 4) * 4 + y if slot < 3 else z * 4 + lax.rem(y + far, 4)
            for s in range(3):
                part = pl.ds(64 * s, 64)
                mask = struct[1, lax.div(((x * 2 + k) * 16 + place) * 3 + s, 2)].astype(jnp.float32)
                near_lead[slot, part] = near_lead[slot, part] * mask
        for slot in range(8):
            rows_in = near_lead[slot] if slot < 6 else lead[7 - slot]
            turned_h[slot], turned_l[slot] = split(jnp.transpose(rows_in))
        link_h[...], link_l[...] = split(link[...])
        knil_h[...], knil_l[...] = split(jnp.transpose(link[...]))

    def pick(h):
        return (prod_a, got_a, far_a) if h == 0 else (prod_b, got_b, far_b)

    def roles(h, unit):
        dy, dz = unit
        near, far = (dy, dz) if h == 0 else (dz, dy)
        return near, far, *route(near, far)

    def next_to(h, way, phase=1):
        along_y = (h == 0) == (phase == 1)
        return at(dy=way) if along_y else at(dz=way)

    def hop(p, h, unit):
        near, far, kind, way = roles(h, unit)
        prod, got, _ = pick(h)
        slot = 0 if kind == "relay" else (1 if way == 1 else 2)
        return remote(
            prod.at[p, PLACE[unit]], got.at[p, slot, far], r_send.at[p, h], r_recv.at[p, min(slot, 1), far],
            next_to(h, way),
        )

    def hop_wait(p, kind, far):
        ref = got_a.at[p, 0] if kind else got_a.at[p, pl.ds(0, 2), far]
        remote(ref, ref, r_send.at[p, 0], r_recv.at[p, kind, far], at(dk=1)).wait_recv()

    def unit_of(h, near, far):
        return (near, far) if h == 0 else (far, near)

    def compute(p, lo, hi):
        @pl.loop(lo, hi)
        def _(u):
            if p == 0:
                for v in range(lo, hi):

                    @pl.when(u == v)
                    def _(v=v):
                        t_copy(v).wait()

            high, low = split(t_buf[u])
            wide = (dot(high, lead_h[p]) + dot(low, lead_h[p])) + dot(high, lead_l[p])
            prod_a[p, u] = wide[:, :HALF]
            prod_b[p, u] = wide[:, HALF:]
            for v in range(lo, hi):
                sends = [h for h in range(2) if roles(h, UNITS[v])[2] in ("relay", "own")]
                if sends:

                    @pl.when(u == v)
                    def _(v=v, sends=sends):
                        for h in sends:
                            hop(p, h, UNITS[v]).start()

    def joined(p, far):
        hop_wait(p, 0, far)
        for h in range(2):
            prod, got, _ = pick(h)
            unit = unit_of(h, 1 if far % 2 == 0 else 3, far)
            prod[p, PLACE[unit]] = prod[p, PLACE[unit]] + got[p, 0, far]
            hop(p, h, unit).start()

    def second_send(p, h, m):
        prod, _, got = pick(h)
        if p == 0:
            far = m + 1
            return remote(
                prod.at[p, PLACE[unit_of(h, 0, far)]], got.at[p, m], f_send.at[p, h], f_recv.at[p, 0],
                next_to(h, far, phase=2),
            )
        far, way, lo, n = ((2, 1, 0, 96), (2, -1, 96, 96), (1, 1, 0, ROWS), (3, -1, 0, ROWS))[m]
        part = pl.ds(lo, n)
        return remote(
            prod.at[p, PLACE[unit_of(h, 0, far)], part], got.at[p, max(0, m - 1), part], f_send.at[p, h],
            f_recv.at[p, min(m, 2)], next_to(h, way, phase=2),
        )

    def second_wait(p, m):
        if m < 2:
            ref = far_a.at[p, 0]
        else:
            ref = got_a.at[p, pl.ds(0, 2), pl.ds(0, 3)] if p == 0 else got_a.at[p, 0]
        remote(ref, ref, f_send.at[p, 0], f_recv.at[p, m if p else 0], at(dk=1)).wait_recv()

    def second_phase(p, far):
        hop_wait(p, 1, far)
        for h in range(2):
            prod, got, _ = pick(h)
            u = PLACE[unit_of(h, 0, far)]
            prod[p, u] = prod[p, u] + (got[p, 1, far] + got[p, 2, far])
            if p == 0 and far:
                second_send(p, h, far - 1).start()
            if p == 1 and far == 2:
                second_send(p, h, 0).start()
                second_send(p, h, 1).start()

    def gain(far):
        for h in range(2):
            prod, _, _ = pick(h)
            slot = 6 if far == 0 else far - 1 + 3 * h
            part = three((turned_h[slot], turned_l[slot]), split(prod[1, PLACE[unit_of(h, 0, far)]]))
            cols = pl.ds(h * HALF, HALF)
            tail[:, cols] = part if far == 2 else tail[:, cols] + part

    def pass_on(far):
        m = far // 2
        second_wait(1, m)
        for h in range(2):
            prod, _, got = pick(h)
            u = PLACE[unit_of(h, 0, far)]
            part = pl.ds(96 * m, 96)
            prod[1, u, part] = prod[1, u, part] + got[1, 0, part]
            second_send(1, h, 2 + m).start()

    def finish(p):
        second_wait(p, 2)
        for h in range(2):
            prod, _, got = pick(h)
            value = prod[p, PLACE[(0, 0)]]
            if p == 0:
                value = (value + got[p, 0]) + (got[p, 1] + got[p, 2])
            else:
                value = value + (got[p, 1] + got[p, 2])
            y_buf[p, :, pl.ds(h * HALF, HALF)] = value

    def rows(ref, start, size):
        return ref.at[pl.ds(pl.multiple_of(start, 8), size)]

    def sent(src, dst, i, where):
        return remote(src, dst, s_send.at[i], s_recv.at[i], where)

    def spot(ref, start, place):
        row = pl.multiple_of(start + 8 * lax.div(place, 2), 8)
        return ref.at[pl.ds(row, 8), pl.ds(pl.multiple_of(lax.rem(place, 2) * HALF, HALF), HALF)]

    quart = k * W + x * 64

    def early_swap(core):
        return sent(rows(sums, core * W, W), sum_p, 0, at(dk=1))

    def early_x(dx):
        there = lax.rem(x + dx, 4)
        return sent(rows(sums, k * W + there * 64, 64), sum_x.at[dx - 1], 1, at(dx=dx))

    def early_plane(o):
        dz, dy = plane[o]
        where = at(dz=dz, dy=dy)
        return sent(spot(sums, quart, where[2] * 4 + where[3]), sum_q.at[o], 2, where)

    def early_spread(o):
        dz, dy = plane[o]
        mine = spot(total, quart, c)
        return sent(mine, mine, 3, at(dz=dz, dy=dy))

    def early_spread_x(dx):
        mine = rows(total, quart, 64)
        return sent(mine, mine, 4, at(dx=dx))

    def early_back(core):
        half = rows(total, core * W, W)
        return sent(half, half, 5, at(dk=1))

    def early(step):
        if step == 0:
            early_swap(1 - k).start()
        if step == 1:
            early_swap(1 - k).wait_recv()
            half = rows(sums, k * W, W)
            half[...] = half[...] + sum_p[...]
            for dx in (2, 1, 3):
                early_x(dx).start()
        if step == 2:
            sent(sum_x, sum_x, 1, at(dk=1)).wait_recv()
            mine = rows(sums, quart, 64)
            mine[...] = (mine[...] + sum_x[0]) + (sum_x[1] + sum_x[2])
            for o in range(15):
                early_plane(o).start()
        if step == 3:
            sent(sum_q, sum_q, 2, at(dk=1)).wait_recv()
            value = spot(sums, quart, c)[...]
            for o in range(15):
                value = value + sum_q[o]
            spot(total, quart, c)[...] = value
            for o in range(15):
                early_spread(o).start()
        if step == 4:
            sent(sum_q, sum_q, 3, at(dk=1)).wait_recv()
            for dx in (2, 1, 3):
                early_spread_x(dx).start()
        if step == 5:
            sent(sum_x, sum_x, 4, at(dk=1)).wait_recv()
            early_back(k).start()
        if step == 6:
            early_back(1 - k).wait_recv()

    def late_sent(src, dst, i, where):
        return remote(src, dst, e_send.at[i], e_recv.at[i], where)

    def late_swap(core):
        return late_sent(rows(tail, core * HALF, HALF), tail_p, 0, at(dk=1))

    def late_plane(o):
        dz, dy = plane[o]
        where = at(dz=dz, dy=dy)
        return late_sent(rows(tail, k * HALF + 8 * (where[2] * 4 + where[3]), 8), tail_q.at[o], 1, where)

    def late_x(dx):
        return late_sent(tail_x.at[x], tail_x.at[x], 2, at(dx=dx))

    def late_spread(o):
        dz, dy = plane[o]
        mine = rows(last, k * HALF + 8 * c, 8)
        return late_sent(mine, mine, 3, at(dz=dz, dy=dy))

    def late_back(core):
        half = rows(last, core * HALF, HALF)
        return late_sent(half, half, 4, at(dk=1))

    def late(step):
        if step == 0:
            late_swap(1 - k).start()
        if step == 1:
            late_swap(1 - k).wait_recv()
            half = rows(tail, k * HALF, HALF)
            half[...] = half[...] + tail_p[...]
            for o in range(15):
                late_plane(o).start()
        if step == 2:
            late_sent(tail_q, tail_q, 1, at(dk=1)).wait_recv()
            value = rows(tail, k * HALF + 8 * c, 8)[...]
            for o in range(15):
                value = value + tail_q[o]
            tail_x[x] = value
            for dx in (2, 1, 3):
                late_x(dx).start()
        if step == 3:
            three = tail_x.at[pl.ds(0, 3)]
            late_sent(three, three, 2, at(dx=1)).wait_recv()
            rows(last, k * HALF + 8 * c, 8)[...] = (tail_x[0] + tail_x[1]) + (tail_x[2] + tail_x[3])
            for o in range(15):
                late_spread(o).start()
        if step == 4:
            late_sent(tail_q, tail_q, 3, at(dk=1)).wait_recv()
            late_back(k).start()
        if step == 5:
            late_back(1 - k).wait_recv()

    def out_copy(i):
        src = (tall.at[0], square.at[0], tall.at[1], square.at[1], square.at[2])[i]
        dst = (out1, diag1, out2, cross2, diag2)[i]
        return pltpu.make_async_copy(src, dst, out_sem.at[i])

    gather_1(0)
    gather_0(1)
    for slot in (0, 3, 2, 5):
        share(slot).start()
    gather_2(0)
    for slot in (1, 4):
        share(slot).start()
    gather_3(0)
    gather_4(0)
    gather_5(0)
    gather_1(1)
    compute(0, 0, 4)
    compute(0, 4, 7)
    gather_2(1)
    compute(0, 7, 12)
    joined(0, 2)
    gather_3(1)
    compute(0, 12, 14)
    gather_4(1)
    compute(0, 14, 16)
    joined(0, 3)
    joined(0, 1)
    joined(0, 0)
    gather_5(1)
    compute(1, 0, 4)
    second_phase(0, 2)
    compute(1, 4, 7)
    second_phase(0, 3)
    second_phase(0, 1)
    compute(1, 7, 12)
    joined(1, 2)
    second_phase(0, 0)
    compute(1, 12, 16)
    joined(1, 3)
    joined(1, 1)
    joined(1, 0)
    share_done()
    finish(0)
    y_parts = split(y_buf[0])
    for p in range(2):
        sums[pl.ds(p * W, W)] = three((turned_h[7 - p], turned_l[7 - p]), y_parts)
    early(0)
    second_phase(1, 2)
    gain(2)
    early(1)
    second_phase(1, 3)
    gain(3)
    second_phase(1, 1)
    gain(1)
    second_phase(1, 0)
    gain(0)
    late(0)
    tall[0] = -y_buf[0]
    out_copy(0).start()
    early(2)
    late(1)
    pass_on(3)
    pass_on(1)
    tall[1] = exact(y_buf[0], link[...])
    early(3)
    late(2)
    finish(1)
    tall[1] = tall[1] - y_buf[1]
    out_copy(2).start()
    late(3)
    early(4)
    early(5)
    late(4)
    for p in range(2):

        @pl.when(at_home)
        def _(p=p):
            three = raw.at[p, 0, pl.ds(0, 144)]
            remote(three, three, g1_send.at[p], g1_recv.at[p, 0], at(dk=1)).wait_send()

        @pl.when(jnp.logical_not(at_home))
        def _(p=p):
            remote(raw.at[p, 0], raw.at[p, 0], g1_send.at[p], g1_recv.at[p, 0], at(dk=1)).wait_send()

        twelve, sixteen = raw.at[p, pl.ds(0, 3)], raw.at[p, pl.ds(0, 4)]
        remote(twelve, twelve, g2_send.at[p], g2_recv.at[p, 0, 0], at(dk=1)).wait_send()
        remote(sixteen, sixteen, g3_send.at[p], g3_recv.at[p], at(dk=1)).wait_send()
        for h in range(2):
            _, got, final = pick(h)
            remote(got.at[p], got.at[p], r_send.at[p, h], r_recv.at[p, 0, 0], at(dk=1)).wait_send()
            remote(final.at[p], final.at[p], f_send.at[p, h], f_recv.at[p, 0], at(dk=1)).wait_send()
    for ref, i in ((sum_p, 0), (sum_x, 1), (sum_q, 2), (sum_q, 3), (sum_x, 4)):
        sent(ref, ref, i, at(dk=1)).wait_send()
    for ref, i in ((tail_p, 0), (tail_q, 1), (tail_x.at[pl.ds(0, 3)], 2)):
        late_sent(ref, ref, i, at(dk=1)).wait_send()
    late_sent(tail_q, tail_q, 3, at(dk=1)).wait_send()
    remote(near_lead, near_lead, n_sem.at[0], n_sem.at[1], at(dk=1)).wait_send()
    for i in (0, 2):
        out_copy(i).wait()
    early(6)
    square[0] = inv1[...] + total[pl.ds(0, W)]
    out_copy(1).start()
    link_parts, cross_sum = (link_h[...], link_l[...]), total[pl.ds(W, W)]
    square[1] = jnp.transpose(cross_sum) - three(split(square[0]), link_parts)
    out_copy(3).start()
    square[2] = (inv2[...] - three((knil_h[...], knil_l[...]), split(square[1]))) - three(
        split(cross_sum), link_parts
    )
    late(5)
    square[2] = square[2] + last[...]
    out_copy(4).start()
    late_back(k).wait_send()
    sent(sum_p, sum_p, 5, at(dk=1)).wait_send()
    for i in (1, 3, 4):
        out_copy(i).wait()


def write_out(*refs):
    sources, results, held, sems = refs[:5], refs[5:10], refs[10:15], refs[15]
    into = [pltpu.make_async_copy(a, b, sems.at[0, i]) for i, (a, b) in enumerate(zip(sources, held))]
    out = [pltpu.make_async_copy(a, b, sems.at[1, i]) for i, (a, b) in enumerate(zip(held, results))]
    for copy in into:
        copy.start()
    for first, second in zip(into, out):
        first.wait()
        second.start()
    for copy in out:
        copy.wait()


def on_device(trailing, first, second, link, inv1, inv2, struct):
    f32, bf16 = jnp.float32, jnp.bfloat16
    square = jax.ShapeDtypeStruct((W, W), f32)
    tall = jax.ShapeDtypeStruct((ROWS, W), f32)
    anywhere = pl.BlockSpec(memory_space=pl.ANY)
    dma = pltpu.SemaphoreType.DMA
    block = (ROWS, HALF)
    parts = pl.pallas_call(
        kernel,
        out_shape=(tall, square, tall, square, square),
        in_specs=[pl.BlockSpec(memory_space=pltpu.SMEM)] + [anywhere] * 6,
        out_specs=(anywhere,) * 5,
        scratch_shapes=[
            pltpu.VMEM((16, ROWS, DEPTH), f32),
            pltpu.VMEM((2, 8, ROWS, W), f32),
            pltpu.VMEM((2, DEPTH, W), bf16),
            pltpu.VMEM((2, DEPTH, W), bf16),
            pltpu.VMEM((2, 16, *block), f32),
            pltpu.VMEM((2, 16, *block), f32),
            pltpu.VMEM((2, 3, 4, *block), f32),
            pltpu.VMEM((2, 3, 4, *block), f32),
            pltpu.VMEM((2, 3, *block), f32),
            pltpu.VMEM((2, 3, *block), f32),
            pltpu.VMEM((2, ROWS, W), f32),
            pltpu.VMEM((6, ROWS, W), f32),
            pltpu.VMEM((8, W, ROWS), bf16),
            pltpu.VMEM((8, W, ROWS), bf16),
            pltpu.VMEM((W, W), f32),
            pltpu.VMEM((W, W), bf16),
            pltpu.VMEM((W, W), bf16),
            pltpu.VMEM((W, W), bf16),
            pltpu.VMEM((W, W), bf16),
            pltpu.VMEM((W, W), f32),
            pltpu.VMEM((W, W), f32),
            pltpu.VMEM((2, ROWS, W), f32),
            pltpu.VMEM((2 * W, W), f32),
            pltpu.VMEM((W, W), f32),
            pltpu.VMEM((3, 64, W), f32),
            pltpu.VMEM((15, 8, HALF), f32),
            pltpu.VMEM((2 * W, W), f32),
            pltpu.VMEM((W, W), f32),
            pltpu.VMEM((HALF, W), f32),
            pltpu.VMEM((15, 8, W), f32),
            pltpu.VMEM((4, 8, W), f32),
            pltpu.VMEM((W, W), f32),
            pltpu.VMEM((2, ROWS, W), f32),
            pltpu.VMEM((3, W, W), f32),
            dma((16,)), dma((5,)), dma((2,)), dma((2, 4)), dma((2,)), dma((2, 2, 4)), dma((2,)), dma((2,)),
            dma((2,)), dma((2, 2)), dma((2, 2, 4)), dma((2, 2)), dma((2, 3)), dma((6,)), dma((6,)), dma((5,)), dma((5,)),
            dma((5,)),
        ],
        compiler_params=pltpu.CompilerParams(
            collective_id=0, has_side_effects=True, vmem_limit_bytes=60 * 1024 * 1024
        ),
        name="selected_inversion",
    )(struct, trailing, first, second, link, inv1, inv2)
    return pl.pallas_call(
        write_out,
        out_shape=(tall, square, tall, square, square),
        in_specs=[anywhere] * 5,
        out_specs=(anywhere,) * 5,
        scratch_shapes=[pltpu.VMEM(a.shape, f32) for a in (tall, square, tall, square, square)] + [dma((2, 5))],
        compiler_params=pltpu.CompilerParams(vmem_limit_bytes=60 * 1024 * 1024),
        name="write_out",
    )(*parts)


def solution(mesh):
    finer = Mesh(mesh.devices.reshape(4, 2, 4, 4), AXES)
    row, col = ("x", "core"), ("z", "y")
    both = (*row, *col)
    in_specs = (P(row, col), P(both, None), P(both, None), P(), P(), P(), P())
    out_specs = (P(both, None), P(), P(both, None), P(), P())
    return jax.shard_map(on_device, mesh=finer, in_specs=in_specs, out_specs=out_specs, check_vma=False)
```
